32 devices in a mesh: group: 2 (over x), seq: 8 (over z, y), tensor: 2 (over core).
Axes of the slice: x: 2, y: 2, z: 4, core: 2. Of those that a mesh axis runs over, the one named last changes fastest.
Arguments:
- hidden: bfloat16 [6, 1024, 8192], P('group', 'seq', 'tensor'), parts along dimension 0, may hold values from -64 to 64
- norm_gain: bfloat16 [8192], replicated, may hold values from 0.099609375 to 1.8984375
- w_kv: bfloat16 [8192, 1024], P(None, 'tensor'), may hold values from -0.0625 to 0.0625
- lengths: int32 [6], P('group'), parts along dimension 0, may hold values from 512 to 1024
- page_table: int32 [6, 8], P('group', 'seq'), parts along dimension 0, may hold values from 0 to 63, as said below
Outputs:
- kv_cache: bfloat16 [128, 128, 1024], P(('group', 'seq'), None, 'tensor'), parts along dimension 0
The draws below stay inside these ranges and needn't reach their ends.
There are 2 independent parts, one for each index of `group`. The reference program is written for one: setup_inputs(seed, part) draws one part's arguments, and reference() takes and returns one part's arrays. A program takes and returns all parts, laid end to end along the dimension named above; an argument that names none is the same for every part. Nothing has to cross between parts.
Inputs may be any that keep to these rules, and one draw needn't show every extreme that they name: `page_table`: entries are distinct; page p is held by index p // 8 of seq in its slot p % 8. In every draw some index of seq holds 8 pages whose blocks all start below the window's length, and some index of seq sends all its 3 blocks to that one holder.
All inputs are finite; a program needn't handle non-finite values.
Results may differ from the reference program's by a relative error of at most 0.0049.
Values may be sent and summed in bfloat16 or wider, within the bound.
No kernel may reach another device: no remote copies, remote signals or barrier semaphores. Data moves between devices by JAX's collectives and lax.ppermute only.
A program may use at most 128 MiB of HBM per device.

```python
import jax
import jax.numpy as jnp
from jax import lax

D = 8192
HD = 128
KVH = 4
BLOCK = 128
SEQS = 3
BPD = 1
SLOTS = 8
LENGTH = 1024
BLOCKS = 8
PAGES = 64
N_SEQ = 8


def draw_hidden(key, part):
    base = jax.random.fold_in(key, 11)
    key_base, key_rows, key_cols = jax.random.split(base, 3)
    shape = (SEQS, LENGTH, D)
    col_scale = jnp.exp(jax.random.uniform(key_cols, (1, 1, D), jnp.float32, -1.15, 1.15))
    row_scale = jnp.exp(jax.random.uniform(key_rows, (SEQS, LENGTH, 1), jnp.float32, -1.15, 1.15))
    values = jax.random.truncated_normal(key_base, -5.0, 5.0, shape, jnp.float32)
    return (values * row_scale * col_scale).astype(jnp.bfloat16)


def draw_page_table(key, part):
    base = jax.random.fold_in(key, 23)
    key_owner, key_sender, key_bias, key_spread, key_tail, key_order = jax.random.split(base, 6)
    total_blocks = SEQS * BLOCKS
    favoured = jax.random.randint(key_owner, (), 0, N_SEQ)
    sender = jax.random.randint(key_sender, (), 0, N_SEQ // 2)
    owner_bias = jax.random.randint(key_bias, (N_SEQ,), 0, 4)
    page_owner = jnp.arange(PAGES, dtype=jnp.int32) // SLOTS
    spread = jax.random.permutation(key_spread, PAGES).astype(jnp.int32)
    scores = jnp.where(page_owner == favoured, 8 * PAGES, 0) + owner_bias[page_owner] * PAGES + spread
    chosen = lax.top_k(scores, total_blocks)[1].astype(jnp.int32)
    head_pages = chosen[:SLOTS]
    tail_pages = jax.random.permutation(key_tail, chosen[SLOTS:])
    page_list = jnp.concatenate([head_pages, tail_pages]).astype(jnp.int32)
    block_device = jnp.arange(total_blocks, dtype=jnp.int32) % BLOCKS // BPD
    ranking = jnp.where(block_device == sender, 0, jnp.where(block_device < N_SEQ // 2, 1, 2))
    order_key = ranking * total_blocks + jax.random.permutation(key_order, total_blocks).astype(jnp.int32)
    ordering = jnp.argsort(order_key, stable=True)
    table = jnp.zeros((total_blocks,), jnp.int32).at[ordering].set(page_list)
    return table.reshape(SEQS, BLOCKS)


def steps_of(rng, extent, cuts, smallest, largest):
    def one(dim, blocks):
        steps = jax.random.uniform(jax.random.fold_in(jax.random.fold_in(rng, 6), dim), (blocks,), jnp.float32, smallest / len(cuts), largest / len(cuts))
        return jnp.repeat(jnp.exp(steps), extent[dim] // blocks).reshape((-1,) + (1,) * (len(extent) - dim - 1))

    loudness = one(*cuts[0])
    for cut in cuts[1:]:
        loudness = loudness * one(*cut)
    return loudness


def bell_draw(key, extent, width, bound, cuts=(), held_as=jnp.bfloat16):
    entries = jax.random.normal(key, extent, jnp.float32) * width
    if len(cuts) > 0:
        entries = steps_of(key, extent, cuts, -0.22, 0.18) * entries
    return jnp.clip(entries, min=-bound, max=bound).astype(held_as)


def setup_inputs(seed: int = 0, part: int = 0) -> dict:
    arg_keys = jax.random.split(jax.random.key(seed), 6)
    own_keys = jax.random.split(jax.random.fold_in(arg_keys[5], part), 6)
    hidden = draw_hidden(jax.random.fold_in(jax.random.fold_in(arg_keys[5], part), 71), part)
    norm_gain = jnp.clip(1.0 + 0.18 * jax.random.normal(arg_keys[1], (D,), jnp.float32), 0.099609375, 1.8984375).astype(jnp.bfloat16)
    w_kv = bell_draw(arg_keys[2], (D, KVH * 2 * HD), D ** -0.5, 0.0625, ((1, 2),))
    lengths = jax.random.randint(own_keys[3], (SEQS,), LENGTH // 2, LENGTH + 1).astype(jnp.int32)
    page_table = draw_page_table(jax.random.fold_in(jax.random.fold_in(arg_keys[5], part), 71), part)
    return {"hidden": hidden, "norm_gain": norm_gain, "w_kv": w_kv, "lengths": lengths, "page_table": page_table}


epsilon = 1e-05
rope_base = 500000.0

def rotate(key_heads, positions):
    half_dim = key_heads.shape[-1] // 2
    inv_freq = rope_base ** (-2.0 * jnp.arange(half_dim, dtype=jnp.float32) / key_heads.shape[-1])
    angles = positions.astype(jnp.float32)[:, None] * inv_freq[None, :]
    cosine = jnp.cos(angles)[:, None, :]
    sine = jnp.sin(angles)[:, None, :]
    first = key_heads[..., :half_dim]
    second = key_heads[..., half_dim:]
    return jnp.concatenate([first * cosine - second * sine, second * cosine + first * sine], axis=-1)

def reference(hidden, norm_gain, w_kv, lengths, page_table):
    wide_f32 = hidden.astype(jnp.float32)
    mean_sq = lax.optimization_barrier(jnp.sum(wide_f32 * wide_f32, axis=-1, keepdims=True)) / D
    normed = (wide_f32 * lax.rsqrt(mean_sq + epsilon) * norm_gain.astype(jnp.float32)).astype(jnp.bfloat16)
    projected = jnp.dot(normed.reshape(-1, D), w_kv, preferred_element_type=jnp.float32)
    projected = projected.reshape(SEQS, LENGTH, KVH, 2, HD)
    positions = jnp.arange(LENGTH, dtype=jnp.int32)
    rotated = rotate(projected[:, :, :, 0, :], positions)
    stacked = jnp.stack([rotated, projected[:, :, :, 1, :]], axis=3)
    living = (positions[None, :] < lengths[:, None])[:, :, None, None, None]
    restored = jnp.where(living, stacked, jnp.zeros((), jnp.float32)).astype(jnp.bfloat16)
    restored = restored.reshape(SEQS * BLOCKS, BLOCK, KVH * 2 * HD)
    kv_cache = jnp.zeros((PAGES, BLOCK, KVH * 2 * HD), jnp.bfloat16)
    return kv_cache.at[page_table.reshape(-1).astype(jnp.int32)].set(restored)
```

```python
import functools

import jax
import jax.numpy as jnp
from jax import lax
from jax.experimental import pallas as pl
from jax.experimental.pallas import tpu as pltpu
from jax.sharding import PartitionSpec as P

HD = 128
BLOCK = 128
SLOTS = 8
PIECES = 2
DEPTH = 512


epsilon = 1e-05
rope_base = 500000.0


def rotary_tables(positions):
    half_dim = HD // 2
    inv_freq = rope_base ** (-2.0 * jnp.arange(half_dim, dtype=jnp.float32) / HD)
    angles = positions.astype(jnp.float32)[:, None] * inv_freq[None, :]
    cosine = jnp.cos(angles)
    sine = jnp.sin(angles)
    return jnp.concatenate([cosine, cosine], axis=-1), jnp.concatenate([-sine, sine], axis=-1)


def accumulate(x_ref, g_ref, w_ref, acc_ref, sq_ref):
    x = x_ref[...]
    if sq_ref is not None:
        wide = x.astype(jnp.float32)
        wide = wide * wide
        total = sq_ref[...]
        for c in range(x.shape[1] // 128):
            total += wide[:, c * 128 : (c + 1) * 128]
        sq_ref[...] = total
    scaled = (x.astype(jnp.float32) * g_ref[...]).astype(jnp.bfloat16)
    acc_ref[...] += jnp.dot(scaled, w_ref[...], preferred_element_type=jnp.float32)


def first_half_kernel(info_ref, x_ref, g_ref, w_ref, acc_ref, sq_ref):
    @pl.when(pl.program_id(0) == 0)
    def _():
        acc_ref[...] = jnp.zeros_like(acc_ref)
        sq_ref[...] = jnp.zeros_like(sq_ref)

    accumulate(x_ref, g_ref, w_ref, acc_ref, sq_ref)


def first_half(info, x, gain, w):
    rows, width = x.shape
    cols = w.shape[1]
    steps = width // DEPTH
    return pl.pallas_call(
        first_half_kernel,
        grid_spec=pltpu.PrefetchScalarGridSpec(
            num_scalar_prefetch=1,
            grid=(steps,),
            in_specs=[
                pl.BlockSpec((rows, DEPTH), lambda k, info: (0, k)),
                pl.BlockSpec((1, DEPTH), lambda k, info: (0, info[0] * steps + k)),
                pl.BlockSpec((DEPTH, cols), lambda k, info: (info[0] * steps + k, 0)),
            ],
            out_specs=[
                pl.BlockSpec((rows, cols), lambda k, info: (0, 0)),
                pl.BlockSpec((rows, 128), lambda k, info: (0, 0)),
            ],
        ),
        out_shape=[
            jax.ShapeDtypeStruct((rows, cols), jnp.float32),
            jax.ShapeDtypeStruct((rows, 128), jnp.float32),
        ],
        compiler_params=pltpu.CompilerParams(dimension_semantics=("arbitrary",)),
        cost_estimate=pl.CostEstimate(
            flops=2 * rows * width * cols,
            bytes_accessed=2 * (rows * width + width * cols) + 4 * rows * cols,
            transcendentals=0,
        ),
        name="first_half",
    )(info, x, gain, w)


def second_half_kernel(group, full_width, own_sq, *refs):
    info_ref, len_ref, x_ref, g_ref, w_ref, acc_in, norm_in, cos_ref, sin_ref = refs[:9]
    outs = refs[9 : 9 + group]
    rest = refs[9 + group :]
    if own_sq:
        inv_ref, acc_ref, sq_ref, stage = rest
    else:
        acc_ref, stage = rest
        sq_ref = None
    k = pl.program_id(0)

    @pl.when(k == 0)
    def _():
        acc_ref[...] = acc_in[...]
        if own_sq:
            sq_ref[...] = norm_in[...]

    accumulate(x_ref, g_ref, w_ref, acc_ref, sq_ref)

    @pl.when(k == pl.num_programs(0) - 1)
    def _():
        if own_sq:
            squares = jnp.sum(sq_ref[...], axis=-1, keepdims=True)
            inv = jnp.broadcast_to(lax.rsqrt(squares / full_width + epsilon), sq_ref.shape)
            inv_ref[...] = inv
        else:
            inv = norm_in[...]
        seqs = len_ref.shape[0]
        per_seq = acc_ref.shape[0] // seqs
        own_start = info_ref[1]
        row = own_start + lax.broadcasted_iota(jnp.int32, (per_seq, HD), 0)
        cosine = cos_ref[...]
        sine = sin_ref[...]
        chunk = BLOCK // group
        per = per_seq // BLOCK
        for s in range(seqs):
            living = row < len_ref[s]
            inv_s = inv[s * per_seq : (s + 1) * per_seq]
            for h in range(acc_ref.shape[1] // (2 * HD)):
                base = h * 2 * HD
                keys = acc_ref[s * per_seq : (s + 1) * per_seq, base : base + HD] * inv_s
                values = acc_ref[s * per_seq : (s + 1) * per_seq, base + HD : base + 2 * HD] * inv_s
                rotated = keys * cosine + pltpu.roll(keys, HD // 2, 1) * sine
                rotated = jnp.where(living, rotated, 0.0).astype(jnp.bfloat16)
                values = jnp.where(living, values, 0.0).astype(jnp.bfloat16)
                for b in range(per):
                    stage[s * per + b, :, base : base + HD] = rotated[b * BLOCK : (b + 1) * BLOCK]
                    stage[s * per + b, :, base + HD : base + 2 * HD] = values[b * BLOCK : (b + 1) * BLOCK]
        for m in range(group):
            start = pl.multiple_of((info_ref[2] ^ m) * chunk, chunk)
            outs[m][...] = stage[:, pl.ds(start, chunk), :]


def second_half(info, lengths, x, gain, w, acc, norm, cosine, sine, piece, group, own_sq):
    rows, width = x.shape
    full_width = w.shape[0]
    cols = w.shape[1] // PIECES
    steps = width // DEPTH
    blocks = rows // BLOCK
    chunk = BLOCK // group
    whole = lambda k, info, lens: (0, 0)
    out_shape = [jax.ShapeDtypeStruct((blocks, chunk, cols), jnp.bfloat16)] * group
    out_specs = [pl.BlockSpec((blocks, chunk, cols), lambda k, info, lens: (0, 0, 0))] * group
    scratch = [pltpu.VMEM((rows, cols), jnp.float32)]
    if own_sq:
        out_shape.append(jax.ShapeDtypeStruct((rows, 128), jnp.float32))
        out_specs.append(pl.BlockSpec((rows, 128), whole))
        scratch.append(pltpu.VMEM((rows, 128), jnp.float32))
    scratch.append(pltpu.VMEM((blocks, BLOCK, cols), jnp.bfloat16))
    return pl.pallas_call(
        functools.partial(second_half_kernel, group, full_width, own_sq),
        grid_spec=pltpu.PrefetchScalarGridSpec(
            num_scalar_prefetch=2,
            grid=(steps,),
            in_specs=[
                pl.BlockSpec((rows, DEPTH), lambda k, info, lens: (0, k)),
                pl.BlockSpec((1, DEPTH), lambda k, info, lens: (0, (1 - info[0]) * steps + k)),
                pl.BlockSpec((DEPTH, cols), lambda k, info, lens: ((1 - info[0]) * steps + k, piece)),
                pl.BlockSpec((rows, cols), lambda k, info, lens: (0, piece)),
                pl.BlockSpec((rows, 128), whole),
                pl.BlockSpec(cosine.shape, whole),
                pl.BlockSpec(sine.shape, whole),
            ],
            out_specs=out_specs,
            scratch_shapes=scratch,
        ),
        out_shape=out_shape,
        compiler_params=pltpu.CompilerParams(dimension_semantics=("arbitrary",)),
        cost_estimate=pl.CostEstimate(
            flops=2 * rows * width * cols,
            bytes_accessed=2 * (rows * width + width * cols) + 4 * rows * cols,
            transcendentals=0,
        ),
        name=f"second_half_{piece}",
    )(info, lengths, x, gain, w, acc, norm, cosine, sine)


def route_kernel(count, group, table_ref, *refs):
    parts = refs[:count]
    outs = refs[count : count + group]
    pool = refs[count + group]
    blocks = parts[0].shape[0]
    for k in range(count):
        pool[k * blocks : (k + 1) * blocks] = parts[k][...]
    for m in range(group):
        for s in range(SLOTS):
            index = table_ref[m * SLOTS + s]
            got = pool[jnp.maximum(index, 0)]
            outs[m][s] = jnp.where(index >= 0, got, jnp.zeros_like(got))


def route(table, parts, group, piece):
    count = len(parts)
    blocks, chunk, cols = parts[0].shape
    vmem = pl.BlockSpec(memory_space=pltpu.VMEM)
    return pl.pallas_call(
        functools.partial(route_kernel, count, group),
        in_specs=[pl.BlockSpec(memory_space=pltpu.SMEM)] + [vmem] * count,
        out_specs=[vmem] * group,
        out_shape=[jax.ShapeDtypeStruct((SLOTS, chunk, cols), jnp.bfloat16)] * group,
        scratch_shapes=[pltpu.VMEM((count * blocks, chunk, cols), jnp.bfloat16)],
        cost_estimate=pl.CostEstimate(
            flops=0,
            bytes_accessed=2 * (count * blocks + group * SLOTS) * chunk * cols,
            transcendentals=0,
        ),
        name=f"route_{piece}",
    )(table, *parts)


def join_kernel(group, info_ref, *refs):
    parts = refs[:group]
    out = refs[-1]
    chunk = parts[0].shape[1]
    for m in range(group):
        start = pl.multiple_of((info_ref[2] ^ m) * chunk, chunk)
        out[:, pl.ds(start, chunk), :] = parts[m][...]


def join(info, parts, before, piece):
    group = len(parts)
    slots, chunk, cols = parts[0].shape
    span = slots // 2
    in_specs = [pl.BlockSpec((span, chunk, cols), lambda i, info: (i, 0, 0))] * group
    operands = list(parts)
    alias = {}
    if before is not None:
        in_specs.append(pl.BlockSpec(memory_space=pl.ANY))
        operands.append(before)
        alias = {1 + group: 0}
    return pl.pallas_call(
        functools.partial(join_kernel, group),
        grid_spec=pltpu.PrefetchScalarGridSpec(
            num_scalar_prefetch=1,
            grid=(slots // span,),
            in_specs=in_specs,
            out_specs=pl.BlockSpec((span, BLOCK, cols), lambda i, info: (i, 0, piece)),
        ),
        out_shape=jax.ShapeDtypeStruct((slots, BLOCK, cols * PIECES), jnp.bfloat16),
        input_output_aliases=alias,
        cost_estimate=pl.CostEstimate(
            flops=0, bytes_accessed=4 * slots * BLOCK * cols, transcendentals=0
        ),
        name=f"join_{piece}",
    )(info, *operands)


def per_device(seq_size, hidden, norm_gain, w_kv, lengths, page_table):
    seq_count, row_count, local_width = hidden.shape
    group = min(4, seq_size)
    tensor_index = lax.axis_index("tensor").astype(jnp.int32)
    own_index = lax.axis_index("seq").astype(jnp.int32)
    flat = hidden.reshape(seq_count * row_count, local_width)
    other = lax.ppermute(flat, "tensor", [(0, 1), (1, 0)])

    def swap(array, k):
        return lax.ppermute(array, "seq", [(i, i ^ k) for i in range(seq_size)])

    ids = page_table.reshape(1, -1)
    bit = 1
    while bit < seq_size:
        ids = jnp.concatenate([ids, swap(ids, bit)], axis=0)
        bit *= 2

    info = jnp.stack([tensor_index, own_index * row_count, own_index % group])
    gain = norm_gain.astype(jnp.float32).reshape(1, -1)
    positions = own_index * row_count + jnp.arange(row_count, dtype=jnp.int32)
    cosine, sine = rotary_tables(positions)

    holders = own_index ^ jnp.arange(group, dtype=jnp.int32)
    pages = (holders[:, None] * SLOTS + jnp.arange(SLOTS, dtype=jnp.int32)[None, :]).reshape(-1)
    flat_ids = ids.reshape(-1)
    order = jnp.arange(1, flat_ids.shape[0] + 1, dtype=jnp.int32)
    table = jnp.sum(jnp.where(pages[:, None] == flat_ids[None, :], order[None, :], 0), axis=1) - 1

    acc, squares = first_half(info, flat, gain, w_kv)
    norm = squares
    kv_cache = None
    for piece in range(PIECES):
        outs = second_half(
            info, lengths, other, gain, w_kv, acc, norm, cosine, sine, piece, group, piece == 0
        )
        if piece == 0:
            norm = outs[group]
        parts = [
            outs[k % group] if k == 0 else swap(outs[k % group], k) for k in range(seq_size)
        ]
        sent = route(table, parts, group, piece)
        placed = [sent[0]] + [swap(sent[m], m) for m in range(1, group)]
        kv_cache = join(info, placed, kv_cache, piece)
    return kv_cache


def solution(mesh):
    placed = (P("group", "seq", "tensor"), P(), P(None, "tensor"), P("group"), P("group", "seq"))
    return jax.shard_map(
        functools.partial(per_device, mesh.shape["seq"]),
        mesh=mesh,
        in_specs=placed,
        out_specs=P(("group", "seq"), None, "tensor"),
        check_vma=False,
    )
```

```python
import functools

import jax
import jax.numpy as jnp
from jax import lax
from jax.experimental import pallas as pl
from jax.experimental.pallas import tpu as pltpu
from jax.sharding import PartitionSpec as P

HD = 128
BLOCK = 128
SLOTS = 8
PIECES = 2
DEPTH = 512
VMEM_LIMIT = 16 << 20


epsilon = 1e-05
rope_base = 500000.0


def rotary_tables(positions):
    half_dim = HD // 2
    inv_freq = rope_base ** (-2.0 * jnp.arange(half_dim, dtype=jnp.float32) / HD)
    angles = positions.astype(jnp.float32)[:, None] * inv_freq[None, :]
    cosine = jnp.cos(angles)
    sine = jnp.sin(angles)
    return jnp.concatenate([cosine, cosine], axis=-1), jnp.concatenate([-sine, sine], axis=-1)


VMEM = pl.BlockSpec(memory_space=pltpu.VMEM)
SMEM = pl.BlockSpec(memory_space=pltpu.SMEM)
ANY = pl.BlockSpec(memory_space=pl.ANY)
HBM = pl.BlockSpec(memory_space=pltpu.HBM)


def near(array):
    return pltpu.with_memory_space_constraint(array, pltpu.VMEM)


def far_away(array):
    return pltpu.with_memory_space_constraint(array, pltpu.HBM)


def lane_squares(x):
    wide = x.astype(jnp.float32)
    wide = wide * wide
    total = wide[:, :128]
    for c in range(1, x.shape[1] // 128):
        total += wide[:, c * 128 : (c + 1) * 128]
    return total


def scaled_by(x, gain):
    return (x.astype(jnp.float32) * gain).astype(jnp.bfloat16)


def first_half_kernel(x_hbm, g_ref, w_hbm, acc_ref, sq_ref, far_ref, x_buf, w_buf, x_sem, w_sem, far_sem):
    width = x_hbm.shape[1]
    steps = width // DEPTH
    side = lax.axis_index("tensor")
    near_row = pl.multiple_of(side * width, width)
    far_row = pl.multiple_of((1 - side) * width, width)
    copies = []
    for k in range(steps):
        span = slice(k * DEPTH, (k + 1) * DEPTH)
        copies.append(
            (
                pltpu.make_async_copy(x_hbm.at[:, span], x_buf.at[:, span], x_sem.at[k]),
                pltpu.make_async_copy(
                    w_hbm.at[pl.ds(near_row + k * DEPTH, DEPTH)], w_buf.at[span], w_sem.at[k]
                ),
            )
        )
    far = pltpu.make_async_copy(w_hbm.at[pl.ds(far_row, width)], far_ref, far_sem)
    for x_copy, w_copy in copies:
        x_copy.start()
        w_copy.start()
    far.start()
    for k in range(steps):
        for copy in copies[k]:
            copy.wait()
        span = slice(k * DEPTH, (k + 1) * DEPTH)
        x = x_buf[:, span]
        gain = g_ref[:, pl.ds(near_row + k * DEPTH, DEPTH)]
        part = jnp.dot(scaled_by(x, gain), w_buf[span], preferred_element_type=jnp.float32)
        squares = lane_squares(x)
        if k == 0:
            acc_ref[...] = part
            sq_ref[...] = squares
        else:
            acc_ref[...] += part
            sq_ref[...] += squares
    far.wait()


def first_half(x, gain, w):
    rows, width = x.shape
    cols = w.shape[1]
    steps = width // DEPTH
    return pl.pallas_call(
        first_half_kernel,
        in_specs=[HBM, VMEM, HBM],
        out_specs=[VMEM, VMEM, VMEM],
        out_shape=[
            pltpu.VMEM((rows, cols), jnp.float32),
            pltpu.VMEM((rows, 128), jnp.float32),
            pltpu.VMEM((width, cols), jnp.bfloat16),
        ],
        scratch_shapes=[
            pltpu.VMEM((rows, width), jnp.bfloat16),
            pltpu.VMEM((width, cols), jnp.bfloat16),
            pltpu.SemaphoreType.DMA((steps,)),
            pltpu.SemaphoreType.DMA((steps,)),
            pltpu.SemaphoreType.DMA,
        ],
        compiler_params=pltpu.CompilerParams(vmem_limit_bytes=VMEM_LIMIT),
        cost_estimate=pl.CostEstimate(
            flops=2 * rows * width * cols,
            bytes_accessed=2 * (rows * width + 2 * width * cols) + 4 * rows * cols,
            transcendentals=0,
        ),
        name="first_half",
    )(far_away(x), gain, far_away(w))


def second_half_kernel(group, piece, len_ref, x_ref, g_ref, w_ref, acc_in, norm_in, cos_ref, sin_ref, *refs):
    outs = refs[:group]
    stage = refs[-1]
    rows, width = x_ref.shape
    seqs = len_ref.shape[0]
    cols = stage.shape[2]
    side = lax.axis_index("tensor")
    own_index = lax.axis_index("seq")
    far_row = pl.multiple_of((1 - side) * width, width)
    lanes = slice(piece * cols, (piece + 1) * cols)
    acc = acc_in[:, lanes]
    squares = norm_in[...]
    for k in range(width // DEPTH):
        span = slice(k * DEPTH, (k + 1) * DEPTH)
        x = x_ref[:, span]
        gain = g_ref[:, pl.ds(far_row + k * DEPTH, DEPTH)]
        acc += jnp.dot(scaled_by(x, gain), w_ref[span, lanes], preferred_element_type=jnp.float32)
        if piece == 0:
            squares += lane_squares(x)
    if piece == 0:
        total = jnp.sum(squares, axis=-1, keepdims=True)
        inv = jnp.broadcast_to(lax.rsqrt(total / g_ref.shape[1] + epsilon), squares.shape)
        refs[group][...] = inv
    else:
        inv = squares
    per_seq = rows // seqs
    row = own_index * per_seq + lax.broadcasted_iota(jnp.int32, (per_seq, HD), 0)
    cosine = cos_ref[...]
    sine = sin_ref[...]
    chunk = BLOCK // group
    per = per_seq // BLOCK
    for s in range(seqs):
        living = row < len_ref[s]
        band = slice(s * per_seq, (s + 1) * per_seq)
        inv_s = inv[band]
        for base in range(0, cols, 2 * HD):
            keys = acc[band, base : base + HD] * inv_s
            values = acc[band, base + HD : base + 2 * HD] * inv_s
            rotated = keys * cosine + pltpu.roll(keys, HD // 2, 1) * sine
            rotated = jnp.where(living, rotated, 0.0).astype(jnp.bfloat16)
            values = jnp.where(living, values, 0.0).astype(jnp.bfloat16)
            for b in range(per):
                part = slice(b * BLOCK, (b + 1) * BLOCK)
                stage[s * per + b, :, base : base + HD] = rotated[part]
                stage[s * per + b, :, base + HD : base + 2 * HD] = values[part]
    for m in range(group):
        start = pl.multiple_of((lax.rem(own_index, group) ^ m) * chunk, chunk)
        outs[m][...] = stage[:, pl.ds(start, chunk), :]


def second_half(lengths, x, gain, w, acc, norm, cosine, sine, piece, group):
    rows, width = x.shape
    cols = w.shape[1] // PIECES
    blocks = rows // BLOCK
    out_shape = [pltpu.VMEM((blocks, BLOCK // group, cols), jnp.bfloat16)] * group
    if piece == 0:
        out_shape.append(pltpu.VMEM((rows, 128), jnp.float32))
    return pl.pallas_call(
        functools.partial(second_half_kernel, group, piece),
        in_specs=[SMEM] + [VMEM] * 7,
        out_specs=[VMEM] * len(out_shape),
        out_shape=out_shape,
        scratch_shapes=[pltpu.VMEM((blocks, BLOCK, cols), jnp.bfloat16)],
        compiler_params=pltpu.CompilerParams(vmem_limit_bytes=VMEM_LIMIT),
        cost_estimate=pl.CostEstimate(
            flops=2 * rows * width * cols,
            bytes_accessed=2 * (rows * width + width * cols) + 4 * rows * cols,
            transcendentals=0,
        ),
        name=f"second_half_{piece}",
    )(lengths, near(x), gain, near(w), near(acc), near(norm), cosine, sine)


def route_kernel(count, group, table_ref, *refs):
    parts = refs[:count]
    outs = refs[count : count + group]
    pool = refs[count + group]
    blocks = parts[0].shape[0]
    for k in range(count):
        pool[k * blocks : (k + 1) * blocks] = parts[k][...]
    for m in range(group):
        for s in range(SLOTS):
            index = table_ref[m * SLOTS + s]
            got = pool[jnp.maximum(index, 0)]
            outs[m][s] = jnp.where(index >= 0, got, jnp.zeros_like(got))


def route(table, parts, group, piece):
    count = len(parts)
    blocks, chunk, cols = parts[0].shape
    return pl.pallas_call(
        functools.partial(route_kernel, count, group),
        in_specs=[SMEM] + [VMEM] * count,
        out_specs=[VMEM] * group,
        out_shape=[pltpu.VMEM((SLOTS, chunk, cols), jnp.bfloat16)] * group,
        scratch_shapes=[pltpu.VMEM((count * blocks, chunk, cols), jnp.bfloat16)],
        compiler_params=pltpu.CompilerParams(vmem_limit_bytes=VMEM_LIMIT),
        cost_estimate=pl.CostEstimate(
            flops=0,
            bytes_accessed=2 * (count * blocks + group * SLOTS) * chunk * cols,
            transcendentals=0,
        ),
        name=f"route_{piece}",
    )(table, *[near(part) for part in parts])


def join(parts, before, piece):
    group = len(parts)
    slots, chunk, cols = parts[0].shape

    def body(*refs):
        out, buf, sem = refs[-3:]
        own = lax.rem(lax.axis_index("seq"), group)
        copies = []
        for s in range(slots):
            for m in range(group):
                start = pl.multiple_of((own ^ m) * chunk, chunk)
                buf[s, pl.ds(start, chunk), :] = refs[m][s]
            copy = pltpu.make_async_copy(
                buf.at[s], out.at[s, :, pl.ds(piece * cols, cols)], sem.at[s]
            )
            copy.start()
            copies.append(copy)
        for copy in copies:
            copy.wait()

    operands = [near(part) for part in parts]
    in_specs = [VMEM] * group
    alias = {}
    if before is not None:
        in_specs.append(ANY)
        operands.append(before)
        alias = {group: 0}
    return pl.pallas_call(
        body,
        in_specs=in_specs,
        out_specs=ANY,
        out_shape=jax.ShapeDtypeStruct((slots, BLOCK, cols * PIECES), jnp.bfloat16),
        scratch_shapes=[
            pltpu.VMEM((slots, BLOCK, cols), jnp.bfloat16),
            pltpu.SemaphoreType.DMA((slots,)),
        ],
        input_output_aliases=alias,
        compiler_params=pltpu.CompilerParams(vmem_limit_bytes=VMEM_LIMIT),
        cost_estimate=pl.CostEstimate(
            flops=0, bytes_accessed=4 * slots * BLOCK * cols, transcendentals=0
        ),
        name=f"join_{piece}",
    )(*operands)


def page_positions(page_table, own_index, group, seq_size, swap):
    ids = page_table.reshape(1, -1)
    bit = 1
    while bit < seq_size:
        ids = jnp.concatenate([ids, swap(ids, bit)], axis=0)
        bit *= 2
    holders = own_index ^ jnp.arange(group, dtype=jnp.int32)
    pages = (holders[:, None] * SLOTS + jnp.arange(SLOTS, dtype=jnp.int32)[None, :]).reshape(-1)
    flat_ids = ids.reshape(-1)
    order = jnp.arange(1, flat_ids.shape[0] + 1, dtype=jnp.int32)
    return jnp.sum(jnp.where(pages[:, None] == flat_ids[None, :], order[None, :], 0), axis=1) - 1


def per_device(seq_size, hidden, norm_gain, w_kv, lengths, page_table):
    seq_count, row_count, local_width = hidden.shape
    group = min(4, seq_size)
    own_index = lax.axis_index("seq").astype(jnp.int32)
    flat = hidden.reshape(seq_count * row_count, local_width)
    other = lax.ppermute(flat, "tensor", [(0, 1), (1, 0)])

    def swap(array, k):
        return lax.ppermute(array, "seq", [(i, i ^ k) for i in range(seq_size)])

    positions = own_index * row_count + jnp.arange(row_count, dtype=jnp.int32)
    cosine, sine = rotary_tables(positions)
    gain = norm_gain.reshape(1, -1)
    flat, gain, cosine, sine = lax.optimization_barrier((flat, gain, cosine, sine))
    acc, norm, far = first_half(flat, gain, w_kv)

    kv_cache = None
    for piece in range(PIECES):
        outs = second_half(lengths, other, gain, far, acc, norm, cosine, sine, piece, group)
        if piece == 0:
            norm = outs[group]
            page_table, own_index, norm = lax.optimization_barrier((page_table, own_index, norm))
            table = page_positions(page_table, own_index, group, seq_size, swap)
        parts = [outs[0]] + [swap(outs[k % group], k) for k in range(1, seq_size)]
        sent = route(table, parts, group, piece)
        placed = [sent[0]] + [swap(sent[m], m) for m in range(1, group)]
        kv_cache = join(placed, kv_cache, piece)
    return kv_cache


def solution(mesh):
    placed = (P("group", "seq", "tensor"), P(), P(None, "tensor"), P("group"), P("group", "seq"))
    return jax.shard_map(
        functools.partial(per_device, mesh.shape["seq"]),
        mesh=mesh,
        in_specs=placed,
        out_specs=P(("group", "seq"), None, "tensor"),
        check_vma=False,
    )
```

```python
import functools

import jax
import jax.numpy as jnp
from jax import lax
from jax.experimental import pallas as pl
from jax.experimental.pallas import tpu as pltpu
from jax.sharding import PartitionSpec as P


HD = 128
BLOCK = 128
SLOTS = 8
LABEL_ROWS = 8
PIECES = 2
DEPTH = 512
VMEM_LIMIT = 16 << 20


epsilon = 1e-05
rope_base = 500000.0


def rotary_tables(positions):
    half_dim = HD // 2
    inv_freq = rope_base ** (-2.0 * jnp.arange(half_dim, dtype=jnp.float32) / HD)
    angles = positions.astype(jnp.float32)[:, None] * inv_freq[None, :]
    cosine = jnp.cos(angles)
    sine = jnp.sin(angles)
    return jnp.concatenate([cosine, cosine], axis=-1), jnp.concatenate([-sine, sine], axis=-1)


VMEM = pl.BlockSpec(memory_space=pltpu.VMEM)
SMEM = pl.BlockSpec(memory_space=pltpu.SMEM)
ANY = pl.BlockSpec(memory_space=pl.ANY)
HBM = pl.BlockSpec(memory_space=pltpu.HBM)


def near(array):
    return pltpu.with_memory_space_constraint(array, pltpu.VMEM)


def far_away(array):
    return pltpu.with_memory_space_constraint(array, pltpu.HBM)


def lane_squares(x):
    wide = x.astype(jnp.float32)
    wide = wide * wide
    total = wide[:, :128]
    for c in range(1, x.shape[1] // 128):
        total += wide[:, c * 128 : (c + 1) * 128]
    return total


def scaled_by(x, gain_ref, row):
    parts = []
    for c in range(x.shape[1] // 128):
        gain = gain_ref[pl.ds(row + c, 1), :]
        wide = x[:, c * 128 : (c + 1) * 128].astype(jnp.float32) * gain
        parts.append(wide.astype(jnp.bfloat16))
    return jnp.concatenate(parts, axis=1)


def first_half_kernel(x_hbm, g_hbm, w_hbm, acc_ref, sq_ref, far_ref, gain, g_buf, x_buf, w_buf, x_sem, w_sem, sems):
    width = x_hbm.shape[1]
    steps = width // DEPTH
    side = lax.axis_index("tensor")
    near_row = pl.multiple_of(side * width, width)
    far_row = pl.multiple_of((1 - side) * width, width)
    copies = []
    for k in range(steps):
        span = slice(k * DEPTH, (k + 1) * DEPTH)
        copies.append(
            (
                pltpu.make_async_copy(x_hbm.at[:, span], x_buf.at[:, span], x_sem.at[k]),
                pltpu.make_async_copy(
                    w_hbm.at[pl.ds(near_row + k * DEPTH, DEPTH)], w_buf.at[span], w_sem.at[k]
                ),
            )
        )
    far = pltpu.make_async_copy(w_hbm.at[pl.ds(far_row, width)], far_ref, sems.at[0])
    gain_copy = pltpu.make_async_copy(g_hbm, g_buf, sems.at[1])
    gain_copy.start()
    for x_copy, w_copy in copies:
        x_copy.start()
        w_copy.start()
    far.start()
    gain_copy.wait()
    gain[...] = g_buf[...].astype(jnp.float32)
    for k in range(steps):
        for copy in copies[k]:
            copy.wait()
        span = slice(k * DEPTH, (k + 1) * DEPTH)
        x = x_buf[:, span]
        scaled = scaled_by(x, gain, side * (width // 128) + k * (DEPTH // 128))
        part = jnp.dot(scaled, w_buf[span], preferred_element_type=jnp.float32)
        squares = lane_squares(x)
        if k == 0:
            acc_ref[...] = part
            sq_ref[...] = squares
        else:
            acc_ref[...] += part
            sq_ref[...] += squares
    far.wait()


def first_half(x, gain, w):
    rows, width = x.shape
    cols = w.shape[1]
    steps = width // DEPTH
    return pl.pallas_call(
        first_half_kernel,
        in_specs=[HBM, HBM, HBM],
        out_specs=[VMEM, VMEM, VMEM, VMEM],
        out_shape=[
            pltpu.VMEM((rows, cols), jnp.float32),
            pltpu.VMEM((rows, 128), jnp.float32),
            pltpu.VMEM((width, cols), jnp.bfloat16),
            pltpu.VMEM(gain.shape, jnp.float32),
        ],
        scratch_shapes=[
            pltpu.VMEM(gain.shape, jnp.bfloat16),
            pltpu.VMEM((rows, width), jnp.bfloat16),
            pltpu.VMEM((width, cols), jnp.bfloat16),
            pltpu.SemaphoreType.DMA((steps,)),
            pltpu.SemaphoreType.DMA((steps,)),
            pltpu.SemaphoreType.DMA((2,)),
        ],
        compiler_params=pltpu.CompilerParams(vmem_limit_bytes=VMEM_LIMIT),
        cost_estimate=pl.CostEstimate(
            flops=2 * rows * width * cols,
            bytes_accessed=2 * (rows * width + 2 * width * cols) + 4 * rows * cols,
            transcendentals=0,
        ),
        name="first_half",
    )(far_away(x), far_away(gain), far_away(w))


def labels_of(page_ref):
    lane = lax.broadcasted_iota(jnp.int32, (LABEL_ROWS, 128), 1)
    tile = jnp.zeros((LABEL_ROWS, 128), jnp.int32)
    for b in range(page_ref.shape[0]):
        tile = jnp.where(lane == 2 * b, page_ref[b] // SLOTS, tile)
        tile = jnp.where(lane == 2 * b + 1, page_ref[b] % SLOTS, tile)
    return tile.astype(jnp.float32).astype(jnp.bfloat16)


def second_half_kernel(group, piece, len_ref, page_ref, x_ref, g_ref, w_ref, acc_in, norm_in, cos_ref, sin_ref, *refs):
    rows, width = x_ref.shape
    seqs = len_ref.shape[0]
    cols = acc_in.shape[1] // PIECES
    tiles = cols // 128
    side = lax.axis_index("tensor")
    own_index = lax.axis_index("seq")
    lanes = slice(piece * cols, (piece + 1) * cols)
    acc = acc_in[:, lanes]
    squares = norm_in[...]
    for k in range(width // DEPTH):
        span = slice(k * DEPTH, (k + 1) * DEPTH)
        x = x_ref[:, span]
        scaled = scaled_by(x, g_ref, (1 - side) * (width // 128) + k * (DEPTH // 128))
        acc += jnp.dot(scaled, w_ref[span, lanes], preferred_element_type=jnp.float32)
        if piece == 0:
            squares += lane_squares(x)
    if piece == 0:
        early, stage, inv_ref = refs[:3]
        total = jnp.sum(squares, axis=-1, keepdims=True)
        inv = jnp.broadcast_to(lax.rsqrt(total / (2 * width) + epsilon), squares.shape)
        inv_ref[...] = inv
    else:
        before, early = refs[:2]
        outs = refs[2 : 2 + group]
        stage = refs[2 + group]
        inv = squares
    per_seq = rows // seqs
    row = own_index * per_seq + lax.broadcasted_iota(jnp.int32, (per_seq, HD), 0)
    cosine = cos_ref[...]
    sine = sin_ref[...]
    chunk = BLOCK // group
    per = per_seq // BLOCK
    for s in range(seqs):
        living = row < len_ref[s]
        band = slice(s * per_seq, (s + 1) * per_seq)
        inv_s = inv[band]
        for tile in range(0, tiles, 2):
            keys = acc[band, tile * HD : (tile + 1) * HD] * inv_s
            values = acc[band, (tile + 1) * HD : (tile + 2) * HD] * inv_s
            rotated = keys * cosine + pltpu.roll(keys, HD // 2, 1) * sine
            rotated = jnp.where(living, rotated, 0.0).astype(jnp.bfloat16)
            values = jnp.where(living, values, 0.0).astype(jnp.bfloat16)
            for b in range(per):
                part = slice(b * BLOCK, (b + 1) * BLOCK)
                stage[s * per + b, tile] = rotated[part]
                stage[s * per + b, tile + 1] = values[part]
    own = lax.rem(own_index, group)
    blocks = stage.shape[0]

    def copy_chunks(out, source, first, stride, member):
        start = pl.multiple_of((own ^ member) * chunk, chunk)
        for b in range(blocks):
            for tile in range(tiles):
                at = (b * stride + first + tile) * chunk
                out[at : at + chunk, :] = source[b, tile, pl.ds(start, chunk), :]

    copy_chunks(early, stage, 0, tiles, 0)
    if piece == 0:
        early[-LABEL_ROWS:, :] = labels_of(page_ref)
    else:
        for m in range(group):
            copy_chunks(outs[m], before, 0, PIECES * tiles, m)
            copy_chunks(outs[m], stage, tiles, PIECES * tiles, m)
            outs[m][-LABEL_ROWS:, :] = labels_of(page_ref)


def second_half(lengths, pages, x, gain, w, acc, norm, cosine, sine, group, before=None):
    rows, width = x.shape
    piece = 0 if before is None else 1
    cols = w.shape[1] // PIECES
    blocks = rows // BLOCK
    tiles = cols // 128
    half = blocks * tiles * (BLOCK // group)
    stage = pltpu.VMEM((blocks, tiles, BLOCK, 128), jnp.bfloat16)
    scratch = []
    operands = [lengths, pages, near(x), near(gain), near(w), near(acc), near(norm), cosine, sine]
    if piece == 0:
        out_shape = [
            pltpu.VMEM((half + LABEL_ROWS, 128), jnp.bfloat16),
            stage,
            pltpu.VMEM((rows, 128), jnp.float32),
        ]
    else:
        operands.append(near(before))
        out_shape = [pltpu.VMEM((half, 128), jnp.bfloat16)]
        out_shape += [pltpu.VMEM((PIECES * half + LABEL_ROWS, 128), jnp.bfloat16)] * group
        scratch.append(stage)
    return pl.pallas_call(
        functools.partial(second_half_kernel, group, piece),
        in_specs=[SMEM] * 2 + [VMEM] * (len(operands) - 2),
        out_specs=[VMEM] * len(out_shape),
        out_shape=out_shape,
        scratch_shapes=scratch,
        compiler_params=pltpu.CompilerParams(vmem_limit_bytes=VMEM_LIMIT),
        cost_estimate=pl.CostEstimate(
            flops=2 * rows * width * cols,
            bytes_accessed=2 * (rows * width + width * cols) + 4 * rows * cols,
            transcendentals=0,
        ),
    )(*operands)


def route_kernel(cuts, group, blocks, *refs):
    count = sum(cuts)
    parts = refs[:count]
    outs = refs[count : count + group]
    pool, label_buf, label_ref, table, sem = refs[count + group :]
    _, tiles, chunk, _ = pool.shape
    at = 0
    for k, cut in enumerate(cuts):
        label_buf[k : k + 1, :] = parts[at][-LABEL_ROWS:, :].astype(jnp.float32)[:1].astype(jnp.int32)
        at += cut
    copy = pltpu.make_async_copy(label_buf, label_ref, sem)
    copy.start()
    at = 0
    for k, cut in enumerate(cuts):
        span = tiles // cut
        for piece in range(cut):
            for b in range(blocks):
                for tile in range(span):
                    row = (b * span + tile) * chunk
                    pool[k * blocks + b, piece * span + tile] = parts[at + piece][row : row + chunk, :]
        at += cut
    for i in range(group * SLOTS):
        table[i] = -1
    copy.wait()
    own_index = lax.axis_index("seq")
    for k in range(len(cuts)):
        for b in range(blocks):
            member = label_ref[k, 2 * b] ^ own_index
            slot = label_ref[k, 2 * b + 1]

            @pl.when(member < group)
            def _():
                table[member * SLOTS + slot] = k * blocks + b

    for m in range(group):
        for s in range(SLOTS):
            index = table[m * SLOTS + s]
            got = pool[jnp.maximum(index, 0)]
            outs[m][s] = jnp.where(index >= 0, got, jnp.zeros_like(got))


def route(parts, group, blocks):
    cuts = tuple(len(part) for part in parts)
    flat = [near(array) for part in parts for array in part]
    chunk = BLOCK // group
    tiles = (parts[0][0].shape[0] - LABEL_ROWS) // (blocks * chunk)
    count = len(cuts)
    return pl.pallas_call(
        functools.partial(route_kernel, cuts, group, blocks),
        in_specs=[VMEM] * len(flat),
        out_specs=[VMEM] * group,
        out_shape=[pltpu.VMEM((SLOTS, tiles, chunk, 128), jnp.bfloat16)] * group,
        scratch_shapes=[
            pltpu.VMEM((count * blocks, tiles, chunk, 128), jnp.bfloat16),
            pltpu.VMEM((count, 128), jnp.int32),
            pltpu.SMEM((count, 128), jnp.int32),
            pltpu.SMEM((group * SLOTS,), jnp.int32),
            pltpu.SemaphoreType.DMA,
        ],
        compiler_params=pltpu.CompilerParams(vmem_limit_bytes=VMEM_LIMIT),
        cost_estimate=pl.CostEstimate(
            flops=0,
            bytes_accessed=256 * (count * blocks + group * SLOTS) * tiles * chunk,
            transcendentals=0,
        ),
        name="route",
    )(*flat)


def join_kernel(*refs):
    out, buf, sems = refs[-3:]
    parts = refs[:-3]
    group = len(parts)
    slots, tiles, chunk, _ = parts[0].shape
    own = lax.rem(lax.axis_index("seq"), group)
    copies = []
    for s in range(slots):
        for m in range(group):
            start = pl.multiple_of((own ^ m) * chunk, chunk)
            for tile in range(tiles):
                buf[s, pl.ds(start, chunk), tile * 128 : (tile + 1) * 128] = parts[m][s, tile]
        copy = pltpu.make_async_copy(buf.at[s], out.at[s], sems.at[s])
        copy.start()
        copies.append(copy)
    for copy in copies:
        copy.wait()


def join(parts):
    slots, tiles, _, _ = parts[0].shape
    shape = (slots, BLOCK, tiles * 128)
    return pl.pallas_call(
        join_kernel,
        in_specs=[VMEM] * len(parts),
        out_specs=ANY,
        out_shape=jax.ShapeDtypeStruct(shape, jnp.bfloat16),
        scratch_shapes=[pltpu.VMEM(shape, jnp.bfloat16), pltpu.SemaphoreType.DMA((slots,))],
        compiler_params=pltpu.CompilerParams(vmem_limit_bytes=VMEM_LIMIT),
        cost_estimate=pl.CostEstimate(
            flops=0, bytes_accessed=4 * slots * BLOCK * tiles * 128, transcendentals=0
        ),
        name="join",
    )(*[near(part) for part in parts])


def per_device(seq_size, hidden, norm_gain, w_kv, lengths, page_table):
    seq_count, row_count, local_width = hidden.shape
    group = min(4, seq_size)
    own_index = lax.axis_index("seq").astype(jnp.int32)
    flat = hidden.reshape(seq_count * row_count, local_width)
    other = lax.ppermute(flat, "tensor", [(0, 1), (1, 0)])

    def swap(array, k):
        return lax.ppermute(array, "seq", [(i, i ^ k) for i in range(seq_size)])

    positions = own_index * row_count + jnp.arange(row_count, dtype=jnp.int32)
    cosine, sine = rotary_tables(positions)
    gain = norm_gain.reshape(-1, 128)
    pages = page_table.reshape(-1)
    flat, cosine, sine = lax.optimization_barrier((flat, cosine, sine))
    acc, squares, far, gain = first_half(flat, gain, w_kv)
    shared = (cosine, sine, group)
    early, before, inv = second_half(lengths, pages, other, gain, far, acc, squares, *shared)
    parts = {}
    if seq_size > group:
        parts[group] = [swap(early, group)]
    late, *outs = second_half(lengths, pages, other, gain, far, acc, inv, *shared, before)
    for k in range(group + 1, seq_size):
        parts[k] = [swap(outs[k % group], k)]
    if seq_size > group:
        parts[group].append(swap(late, group))
    for k in range(1, group):
        parts[k] = [swap(outs[k], k)]
    parts[0] = [outs[0]]
    sent = route([parts[k] for k in range(seq_size)], group, seq_count * row_count // BLOCK)
    placed = [sent[0]]
    for m in range(1, group):
        placed.append(swap(sent[m], m))
    return join(placed)


def solution(mesh):
    placed = (P("group", "seq", "tensor"), P(), P(None, "tensor"), P("group"), P("group", "seq"))

    def body(*operands):
        return per_device(mesh.shape["seq"], *operands)

    return jax.shard_map(
        body,
        mesh=mesh,
        in_specs=placed,
        out_specs=P(("group", "seq"), None, "tensor"),
        check_vma=False,
    )
```

```python
import functools

import jax
import jax.numpy as jnp
from jax import lax
from jax.experimental import pallas as pl
from jax.experimental.pallas import tpu as pltpu
from jax.sharding import PartitionSpec as P


HD = 128
BLOCK = 128
SLOTS = 8
LABEL_ROWS = 8
CUTS = (0, 2, 4)
DEPTH = 512
VMEM_LIMIT = 16 << 20


epsilon = 1e-05
rope_base = 500000.0


def frequencies():
    index = jnp.arange(HD, dtype=jnp.int32).reshape(1, HD) % (HD // 2)
    return rope_base ** (-2.0 * index.astype(jnp.float32) / HD)


VMEM = pl.BlockSpec(memory_space=pltpu.VMEM)
SMEM = pl.BlockSpec(memory_space=pltpu.SMEM)
ANY = pl.BlockSpec(memory_space=pl.ANY)
HBM = pl.BlockSpec(memory_space=pltpu.HBM)


def near(array):
    return pltpu.with_memory_space_constraint(array, pltpu.VMEM)


def far_away(array):
    return pltpu.with_memory_space_constraint(array, pltpu.HBM)


def lane_squares(x):
    wide = x.astype(jnp.float32)
    wide = wide * wide
    total = wide[:, :128]
    for c in range(1, x.shape[1] // 128):
        total += wide[:, c * 128 : (c + 1) * 128]
    return total


def scaled_by(x, gain_ref, row):
    parts = []
    for c in range(x.shape[1] // 128):
        gain = gain_ref[pl.ds(row + c, 1), :]
        wide = x[:, c * 128 : (c + 1) * 128].astype(jnp.float32) * gain
        parts.append(wide.astype(jnp.bfloat16))
    return jnp.concatenate(parts, axis=1)


def first_half_kernel(row_count, x_hbm, g_hbm, w_hbm, freq_ref, acc_ref, sq_ref, far_ref, gain, cos_ref, sin_ref, *scratch):
    g_buf, x_buf, w_buf, x_sem, w_sem, sems = scratch
    width = x_hbm.shape[1]
    steps = width // DEPTH
    side = lax.axis_index("tensor")
    near_row = pl.multiple_of(side * width, width)
    far_row = pl.multiple_of((1 - side) * width, width)
    copies = []
    for k in range(steps):
        span = slice(k * DEPTH, (k + 1) * DEPTH)
        copies.append(
            (
                pltpu.make_async_copy(x_hbm.at[:, span], x_buf.at[:, span], x_sem.at[k]),
                pltpu.make_async_copy(
                    w_hbm.at[pl.ds(near_row + k * DEPTH, DEPTH)], w_buf.at[span], w_sem.at[k]
                ),
            )
        )
    far = pltpu.make_async_copy(w_hbm.at[pl.ds(far_row, width)], far_ref, sems.at[0])
    gain_copy = pltpu.make_async_copy(g_hbm, g_buf, sems.at[1])
    gain_copy.start()
    for x_copy, w_copy in copies:
        x_copy.start()
        w_copy.start()
    far.start()
    first = lax.axis_index("seq") * row_count
    position = first + lax.broadcasted_iota(jnp.int32, cos_ref.shape, 0)
    angle = position.astype(jnp.float32) * freq_ref[...]
    cos_ref[...] = jnp.cos(angle)
    sine = jnp.sin(angle)
    lane = lax.broadcasted_iota(jnp.int32, sine.shape, 1)
    sin_ref[...] = jnp.where(lane < HD // 2, -sine, sine)
    gain_copy.wait()
    gain[...] = g_buf[...].astype(jnp.float32)
    for k in range(steps):
        for copy in copies[k]:
            copy.wait()
        span = slice(k * DEPTH, (k + 1) * DEPTH)
        x = x_buf[:, span]
        scaled = scaled_by(x, gain, side * (width // 128) + k * (DEPTH // 128))
        part = jnp.dot(scaled, w_buf[span], preferred_element_type=jnp.float32)
        squares = lane_squares(x)
        if k == 0:
            acc_ref[...] = part
            sq_ref[...] = squares
        else:
            acc_ref[...] += part
            sq_ref[...] += squares
    far.wait()


def first_half(x, gain, w, freq, row_count):
    rows, width = x.shape
    cols = w.shape[1]
    steps = width // DEPTH
    return pl.pallas_call(
        functools.partial(first_half_kernel, row_count),
        in_specs=[HBM, HBM, HBM, VMEM],
        out_specs=[VMEM] * 6,
        out_shape=[
            pltpu.VMEM((rows, cols), jnp.float32),
            pltpu.VMEM((rows, 128), jnp.float32),
            pltpu.VMEM((width, cols), jnp.bfloat16),
            pltpu.VMEM(gain.shape, jnp.float32),
            pltpu.VMEM((row_count, HD), jnp.float32),
            pltpu.VMEM((row_count, HD), jnp.float32),
        ],
        scratch_shapes=[
            pltpu.VMEM(gain.shape, jnp.bfloat16),
            pltpu.VMEM((rows, width), jnp.bfloat16),
            pltpu.VMEM((width, cols), jnp.bfloat16),
            pltpu.SemaphoreType.DMA((steps,)),
            pltpu.SemaphoreType.DMA((steps,)),
            pltpu.SemaphoreType.DMA((2,)),
        ],
        compiler_params=pltpu.CompilerParams(vmem_limit_bytes=VMEM_LIMIT),
        cost_estimate=pl.CostEstimate(
            flops=2 * rows * width * cols,
            bytes_accessed=2 * (rows * width + 2 * width * cols) + 4 * rows * cols,
            transcendentals=0,
        ),
        name="first_half",
    )(far_away(x), far_away(gain), far_away(w), freq)


def labels_of(page_ref):
    lane = lax.broadcasted_iota(jnp.int32, (LABEL_ROWS, 128), 1)
    tile = jnp.zeros((LABEL_ROWS, 128), jnp.int32)
    for b in range(page_ref.shape[0]):
        tile = jnp.where(lane == 2 * b, page_ref[b] // SLOTS, tile)
        tile = jnp.where(lane == 2 * b + 1, page_ref[b] % SLOTS, tile)
    return tile.astype(jnp.float32).astype(jnp.bfloat16)


def second_half_kernel(group, piece, len_ref, page_ref, x_ref, g_ref, w_ref, acc_in, norm_in, cos_ref, sin_ref, *refs):
    rows, width = x_ref.shape
    seqs = len_ref.shape[0]
    first_tile, last_tile = CUTS[piece], CUTS[piece + 1]
    tiles = last_tile - first_tile
    side = lax.axis_index("tensor")
    own_index = lax.axis_index("seq")
    lanes = slice(first_tile * 128, last_tile * 128)
    acc = acc_in[:, lanes]
    squares = norm_in[...]
    for k in range(width // DEPTH):
        span = slice(k * DEPTH, (k + 1) * DEPTH)
        x = x_ref[:, span]
        scaled = scaled_by(x, g_ref, (1 - side) * (width // 128) + k * (DEPTH // 128))
        acc += jnp.dot(scaled, w_ref[span, lanes], preferred_element_type=jnp.float32)
        if piece == 0:
            squares += lane_squares(x)
    if piece == 0:
        early, stage, inv_ref = refs
        total = jnp.sum(squares, axis=-1, keepdims=True)
        inv = jnp.broadcast_to(lax.rsqrt(total / (2 * width) + epsilon), squares.shape)
        inv_ref[...] = inv
    else:
        before, early = refs[:2]
        outs = refs[2 : 2 + group]
        stage = refs[2 + group]
        inv = squares
    per_seq = rows // seqs
    row = own_index * per_seq + lax.broadcasted_iota(jnp.int32, (per_seq, HD), 0)
    cosine = cos_ref[...]
    sine = sin_ref[...]
    chunk = BLOCK // group
    per = per_seq // BLOCK
    for s in range(seqs):
        living = row < len_ref[s]
        band = slice(s * per_seq, (s + 1) * per_seq)
        inv_s = inv[band]
        for tile in range(tiles):
            made = acc[band, tile * HD : (tile + 1) * HD] * inv_s
            if (first_tile + tile) % 2 == 0:
                made = made * cosine + pltpu.roll(made, HD // 2, 1) * sine
            made = jnp.where(living, made, 0.0).astype(jnp.bfloat16)
            for b in range(per):
                stage[s * per + b, tile] = made[b * BLOCK : (b + 1) * BLOCK]
    own = lax.rem(own_index, group)
    blocks = stage.shape[0]

    def copy_chunks(out, source, first, stride, member):
        start = pl.multiple_of((own ^ member) * chunk, chunk)
        for b in range(blocks):
            for tile in range(source.shape[1]):
                at = (b * stride + first + tile) * chunk
                out[at : at + chunk, :] = source[b, tile, pl.ds(start, chunk), :]

    copy_chunks(early, stage, 0, tiles, 0)
    if piece == 0:
        early[-LABEL_ROWS:, :] = labels_of(page_ref)
    else:
        for m in range(group):
            copy_chunks(outs[m], before, 0, CUTS[-1], m)
            copy_chunks(outs[m], stage, first_tile, CUTS[-1], m)
            outs[m][-LABEL_ROWS:, :] = labels_of(page_ref)


def second_half(lengths, pages, x, gain, w, acc, norm, cosine, sine, group, before=None):
    rows, width = x.shape
    piece = 0 if before is None else 1
    tiles = CUTS[piece + 1] - CUTS[piece]
    blocks = rows // BLOCK
    strip = blocks * (BLOCK // group)
    stage = pltpu.VMEM((blocks, tiles, BLOCK, 128), jnp.bfloat16)
    scratch = []
    operands = [lengths, pages, near(x), near(gain), near(w), near(acc), near(norm), near(cosine), near(sine)]
    if piece == 0:
        out_shape = [
            pltpu.VMEM((tiles * strip + LABEL_ROWS, 128), jnp.bfloat16),
            stage,
            pltpu.VMEM((rows, 128), jnp.float32),
        ]
    else:
        operands.append(near(before))
        out_shape = [pltpu.VMEM((tiles * strip, 128), jnp.bfloat16)]
        out_shape += [pltpu.VMEM((CUTS[-1] * strip + LABEL_ROWS, 128), jnp.bfloat16)] * group
        scratch.append(stage)
    return pl.pallas_call(
        functools.partial(second_half_kernel, group, piece),
        in_specs=[SMEM] * 2 + [VMEM] * (len(operands) - 2),
        out_specs=[VMEM] * len(out_shape),
        out_shape=out_shape,
        scratch_shapes=scratch,
        compiler_params=pltpu.CompilerParams(vmem_limit_bytes=VMEM_LIMIT),
        cost_estimate=pl.CostEstimate(
            flops=2 * rows * width * tiles * 128,
            bytes_accessed=2 * width * (rows + tiles * 128) + 4 * rows * tiles * 128,
            transcendentals=0,
        ),
    )(*operands)


def route_kernel(cuts, group, blocks, *refs):
    count = sum(cuts)
    parts = refs[:count]
    outs = refs[count : count + group]
    pool, label_buf, label_ref, table, sem = refs[count + group :]
    _, _, chunk, _ = pool.shape
    at = 0
    for k, cut in enumerate(cuts):
        label_buf[k : k + 1, :] = parts[at][-LABEL_ROWS:, :].astype(jnp.float32)[:1].astype(jnp.int32)
        at += cut
    copy = pltpu.make_async_copy(label_buf, label_ref, sem)
    copy.start()
    at = 0
    for k, cut in enumerate(cuts):
        first = 0
        for part in parts[at : at + cut]:
            span = part.shape[0] // (blocks * chunk)
            for b in range(blocks):
                for tile in range(span):
                    row = (b * span + tile) * chunk
                    pool[k * blocks + b, first + tile] = part[row : row + chunk, :]
            first += span
        at += cut
    nothing = len(cuts) * blocks
    pool[nothing] = jnp.zeros(pool.shape[1:], pool.dtype)
    wanted = group * SLOTS
    for i in range(wanted):
        table[i] = nothing
    copy.wait()
    own_index = lax.axis_index("seq")
    for k in range(len(cuts)):
        for b in range(blocks):
            member = label_ref[k, 2 * b] ^ own_index
            slot = label_ref[k, 2 * b + 1]
            table[jnp.where(member < group, member * SLOTS + slot, wanted)] = k * blocks + b
    for m in range(group):
        for s in range(SLOTS):
            outs[m][s] = pool[table[m * SLOTS + s]]


def route(parts, group, blocks):
    cuts = tuple(len(part) for part in parts)
    flat = [near(array) for part in parts for array in part]
    chunk = BLOCK // group
    tiles = (parts[0][0].shape[0] - LABEL_ROWS) // (blocks * chunk)
    count = len(cuts)
    return pl.pallas_call(
        functools.partial(route_kernel, cuts, group, blocks),
        in_specs=[VMEM] * len(flat),
        out_specs=[VMEM] * group,
        out_shape=[pltpu.VMEM((SLOTS, tiles, chunk, 128), jnp.bfloat16)] * group,
        scratch_shapes=[
            pltpu.VMEM((count * blocks + 1, tiles, chunk, 128), jnp.bfloat16),
            pltpu.VMEM((count, 128), jnp.int32),
            pltpu.SMEM((count, 128), jnp.int32),
            pltpu.SMEM((group * SLOTS + 1,), jnp.int32),
            pltpu.SemaphoreType.DMA,
        ],
        compiler_params=pltpu.CompilerParams(vmem_limit_bytes=VMEM_LIMIT),
        cost_estimate=pl.CostEstimate(
            flops=0,
            bytes_accessed=256 * (count * blocks + group * SLOTS) * tiles * chunk,
            transcendentals=0,
        ),
        name="route",
    )(*flat)


def join_kernel(members, *refs):
    out, sems = refs[-2:]
    parts = refs[: len(members)]
    _, tiles, chunk, _ = parts[0].shape
    own = lax.rem(lax.axis_index("seq"), BLOCK // chunk)
    copies = []
    for at, m in enumerate(members):
        start = pl.multiple_of((own ^ m) * chunk, chunk)
        for tile in range(tiles):
            there = out.at[:, pl.ds(start, chunk), tile * 128 : (tile + 1) * 128]
            copy = pltpu.make_async_copy(parts[at].at[:, tile], there, sems.at[at, tile])
            copy.start()
            copies.append(copy)
    for copy in copies:
        copy.wait()


def join(parts, members, before=None):
    slots, tiles, chunk, _ = parts[0].shape
    cols = tiles * 128
    operands = [near(part) for part in parts]
    in_specs = [VMEM] * len(parts)
    alias = {}
    if before is not None:
        operands.append(before)
        in_specs.append(ANY)
        alias = {len(parts): 0}
    return pl.pallas_call(
        functools.partial(join_kernel, members),
        in_specs=in_specs,
        out_specs=ANY,
        out_shape=jax.ShapeDtypeStruct((slots, BLOCK, cols), jnp.bfloat16),
        scratch_shapes=[pltpu.SemaphoreType.DMA((len(parts), tiles))],
        input_output_aliases=alias,
        compiler_params=pltpu.CompilerParams(vmem_limit_bytes=VMEM_LIMIT),
        cost_estimate=pl.CostEstimate(
            flops=0, bytes_accessed=4 * len(parts) * slots * chunk * cols, transcendentals=0
        ),
        name="join" if before is None else "join_last",
    )(*operands)


def per_device(seq_size, hidden, norm_gain, w_kv, lengths, page_table):
    seq_count, row_count, local_width = hidden.shape
    group = min(4, seq_size)
    flat = hidden.reshape(seq_count * row_count, local_width)
    other = lax.ppermute(flat, "tensor", [(0, 1), (1, 0)])

    def swap(array, k):
        return lax.ppermute(array, "seq", [(i, i ^ k) for i in range(seq_size)])

    gain = norm_gain.reshape(-1, 128)
    pages = page_table.reshape(-1)
    freq = frequencies()
    flat, freq = lax.optimization_barrier((flat, freq))
    acc, squares, far, gain, cosine, sine = first_half(flat, gain, w_kv, freq, row_count)
    shared = (cosine, sine, group)
    early, before, inv = second_half(lengths, pages, other, gain, far, acc, squares, *shared)
    parts = {k: [] for k in range(seq_size)}

    def send(array, k):
        parts[k].append(swap(array, k))

    if seq_size > group:
        send(early, group)
    late, *outs = second_half(lengths, pages, other, gain, far, acc, inv, *shared, before)
    if seq_size > group:
        send(late, group)
    for k in range(1, seq_size):
        if k != group:
            send(outs[k % group], k)
    parts[0] = [outs[0]]
    sent = route([parts[k] for k in range(seq_size)], group, seq_count * row_count // BLOCK)
    placed = [sent[0]]
    for m in range(1, group):
        placed.append(swap(sent[m], m))
    members = tuple(range(group))
    kv_cache = join(placed[:-1], members[:-1])
    return join(placed[-1:], members[-1:], kv_cache)


def solution(mesh):
    placed = (P("group", "seq", "tensor"), P(), P(None, "tensor"), P("group"), P("group", "seq"))

    def body(*operands):
        return per_device(mesh.shape["seq"], *operands)

    return jax.shard_map(
        body,
        mesh=mesh,
        in_specs=placed,
        out_specs=P(("group", "seq"), None, "tensor"),
        check_vma=False,
    )
```

```python
import functools

import jax
import jax.numpy as jnp
from jax import lax
from jax.experimental import pallas as pl
from jax.experimental.pallas import tpu as pltpu
from jax.sharding import PartitionSpec as P


HD = 128
BLOCK = 128
SLOTS = 8
LABEL_ROWS = 8
DEPTH = 512
VMEM_LIMIT = 16 << 20


epsilon = 1e-05
rope_base = 500000.0


def frequencies():
    index = jnp.arange(HD, dtype=jnp.int32).reshape(1, HD) % (HD // 2)
    return rope_base ** (-2.0 * index.astype(jnp.float32) / HD)


VMEM = pl.BlockSpec(memory_space=pltpu.VMEM)
SMEM = pl.BlockSpec(memory_space=pltpu.SMEM)
ANY = pl.BlockSpec(memory_space=pl.ANY)
HBM = pl.BlockSpec(memory_space=pltpu.HBM)


def near(array):
    return pltpu.with_memory_space_constraint(array, pltpu.VMEM)


def far_away(array):
    return pltpu.with_memory_space_constraint(array, pltpu.HBM)


def lane_squares(x):
    wide = x.astype(jnp.float32)
    wide = wide * wide
    total = wide[:, :128]
    for c in range(1, x.shape[1] // 128):
        total += wide[:, c * 128 : (c + 1) * 128]
    return total


def scaled_by(x, gain_ref, row):
    parts = []
    for c in range(x.shape[1] // 128):
        gain = gain_ref[pl.ds(row + c, 1), :]
        wide = x[:, c * 128 : (c + 1) * 128].astype(jnp.float32) * gain
        parts.append(wide.astype(jnp.bfloat16))
    return jnp.concatenate(parts, axis=1)


def first_half_kernel(row_count, x_hbm, g_hbm, w_hbm, freq_ref, acc_ref, sq_ref, far_ref, gain, cos_ref, sin_ref, *scratch):
    g_buf, x_buf, w_buf, x_sem, w_sem, sems = scratch
    width = x_hbm.shape[1]
    steps = width // DEPTH
    side = lax.axis_index("tensor")
    near_row = pl.multiple_of(side * width, width)
    far_row = pl.multiple_of((1 - side) * width, width)
    copies = []
    for k in range(steps):
        span = slice(k * DEPTH, (k + 1) * DEPTH)
        copies.append(
            (
                pltpu.make_async_copy(x_hbm.at[:, span], x_buf.at[:, span], x_sem.at[k]),
                pltpu.make_async_copy(
                    w_hbm.at[pl.ds(near_row + k * DEPTH, DEPTH)], w_buf.at[span], w_sem.at[k]
                ),
            )
        )
    far = pltpu.make_async_copy(w_hbm.at[pl.ds(far_row, width)], far_ref, sems.at[0])
    gain_copy = pltpu.make_async_copy(g_hbm, g_buf, sems.at[1])
    gain_copy.start()
    for x_copy, w_copy in copies:
        x_copy.start()
        w_copy.start()
    far.start()
    first = lax.axis_index("seq") * row_count
    position = first + lax.broadcasted_iota(jnp.int32, cos_ref.shape, 0)
    angle = position.astype(jnp.float32) * freq_ref[...]
    cos_ref[...] = jnp.cos(angle)
    sine = jnp.sin(angle)
    lane = lax.broadcasted_iota(jnp.int32, sine.shape, 1)
    sin_ref[...] = jnp.where(lane < HD // 2, -sine, sine)
    gain_copy.wait()
    gain[...] = g_buf[...].astype(jnp.float32)
    for k in range(steps):
        for copy in copies[k]:
            copy.wait()
        span = slice(k * DEPTH, (k + 1) * DEPTH)
        x = x_buf[:, span]
        scaled = scaled_by(x, gain, side * (width // 128) + k * (DEPTH // 128))
        part = jnp.dot(scaled, w_buf[span], preferred_element_type=jnp.float32)
        squares = lane_squares(x)
        if k == 0:
            acc_ref[...] = part
            sq_ref[...] = squares
        else:
            acc_ref[...] += part
            sq_ref[...] += squares
    far.wait()


def first_half(x, gain, w, freq, row_count):
    rows, width = x.shape
    cols = w.shape[1]
    steps = width // DEPTH
    return pl.pallas_call(
        functools.partial(first_half_kernel, row_count),
        in_specs=[HBM, HBM, HBM, VMEM],
        out_specs=[VMEM] * 6,
        out_shape=[
            pltpu.VMEM((rows, cols), jnp.float32),
            pltpu.VMEM((rows, 128), jnp.float32),
            pltpu.VMEM((width, cols), jnp.bfloat16),
            pltpu.VMEM(gain.shape, jnp.float32),
            pltpu.VMEM((row_count, HD), jnp.float32),
            pltpu.VMEM((row_count, HD), jnp.float32),
        ],
        scratch_shapes=[
            pltpu.VMEM(gain.shape, jnp.bfloat16),
            pltpu.VMEM((rows, width), jnp.bfloat16),
            pltpu.VMEM((width, cols), jnp.bfloat16),
            pltpu.SemaphoreType.DMA((steps,)),
            pltpu.SemaphoreType.DMA((steps,)),
            pltpu.SemaphoreType.DMA((2,)),
        ],
        compiler_params=pltpu.CompilerParams(vmem_limit_bytes=VMEM_LIMIT),
        cost_estimate=pl.CostEstimate(
            flops=2 * rows * width * cols,
            bytes_accessed=2 * (rows * width + 2 * width * cols) + 4 * rows * cols,
            transcendentals=0,
        ),
        name="first_half",
    )(far_away(x), far_away(gain), far_away(w), freq)


def labels_of(page_ref):
    lane = lax.broadcasted_iota(jnp.int32, (LABEL_ROWS, 128), 1)
    tile = jnp.zeros((LABEL_ROWS, 128), jnp.int32)
    for b in range(page_ref.shape[0]):
        tile = jnp.where(lane == 2 * b, page_ref[b] // SLOTS, tile)
        tile = jnp.where(lane == 2 * b + 1, page_ref[b] % SLOTS, tile)
    return tile.astype(jnp.float32).astype(jnp.bfloat16)


def second_half_kernel(group, members, len_ref, page_ref, x_ref, g_ref, w_ref, acc_in, sq_in, cos_ref, sin_ref, *outs):
    rows, width = x_ref.shape
    per_seq = cos_ref.shape[0]
    per = per_seq // BLOCK
    blocks = rows // BLOCK
    tiles = acc_in.shape[1] // 128
    chunk = BLOCK // group
    side = lax.axis_index("tensor")
    own_index = lax.axis_index("seq")
    own = lax.rem(own_index, group)

    def chunks(ref, columns):
        parts = []
        for m in members:
            for b in range(blocks):
                start = pl.multiple_of(b * BLOCK + (own ^ m) * chunk, chunk)
                parts.append(ref[pl.ds(start, chunk), columns])
        return jnp.concatenate(parts, axis=0)

    acc = chunks(acc_in, slice(None))
    squares = chunks(sq_in, slice(None))
    for k in range(width // DEPTH):
        span = slice(k * DEPTH, (k + 1) * DEPTH)
        x = chunks(x_ref, span)
        scaled = scaled_by(x, g_ref, (1 - side) * (width // 128) + k * (DEPTH // 128))
        acc += jnp.dot(scaled, w_ref[span, :], preferred_element_type=jnp.float32)
        squares += lane_squares(x)
    total = jnp.sum(squares, axis=-1, keepdims=True)
    inv = jnp.broadcast_to(lax.rsqrt(total / (2 * width) + epsilon), squares.shape)
    labels = labels_of(page_ref)
    for i, m in enumerate(members):
        for b in range(blocks):
            at = (i * blocks + b) * chunk
            band = slice(at, at + chunk)
            first = pl.multiple_of(b % per * BLOCK + (own ^ m) * chunk, chunk)
            row = own_index * per_seq + first + lax.broadcasted_iota(jnp.int32, (chunk, HD), 0)
            living = row < len_ref[b // per]
            cosine = cos_ref[pl.ds(first, chunk), :]
            sine = sin_ref[pl.ds(first, chunk), :]
            for tile in range(tiles):
                made = acc[band, tile * HD : (tile + 1) * HD] * inv[band]
                if tile % 2 == 0:
                    made = made * cosine + pltpu.roll(made, HD // 2, 1) * sine
                made = jnp.where(living, made, 0.0).astype(jnp.bfloat16)
                to = (b * tiles + tile) * chunk
                outs[i][to : to + chunk, :] = made
        outs[i][-LABEL_ROWS:, :] = labels


def second_half(lengths, pages, x, gain, w, acc, squares, cosine, sine, group, members):
    rows, width = x.shape
    cols = w.shape[1]
    height = rows // group * (cols // 128) + LABEL_ROWS
    count = rows // group * len(members)
    operands = [near(array) for array in (x, gain, w, acc, squares, cosine, sine)]
    return pl.pallas_call(
        functools.partial(second_half_kernel, group, members),
        in_specs=[SMEM] * 2 + [VMEM] * len(operands),
        out_specs=[VMEM] * len(members),
        out_shape=[pltpu.VMEM((height, 128), jnp.bfloat16)] * len(members),
        compiler_params=pltpu.CompilerParams(vmem_limit_bytes=VMEM_LIMIT),
        cost_estimate=pl.CostEstimate(
            flops=2 * count * width * cols,
            bytes_accessed=2 * width * (count + cols) + 4 * count * cols,
            transcendentals=0,
        ),
    )(lengths, pages, *operands)


def route_kernel(count, group, blocks, *refs):
    parts = refs[:count]
    outs = refs[count : count + group]
    pool, label_buf, label_ref, table, sem = refs[count + group :]
    _, tiles, chunk, _ = pool.shape
    for k in range(count):
        label_buf[k : k + 1, :] = parts[k][-LABEL_ROWS:, :].astype(jnp.float32)[:1].astype(jnp.int32)
    copy = pltpu.make_async_copy(label_buf, label_ref, sem)
    copy.start()
    for k in range(count):
        for b in range(blocks):
            for tile in range(tiles):
                row = (b * tiles + tile) * chunk
                pool[k * blocks + b, tile] = parts[k][row : row + chunk, :]
    nothing = count * blocks
    pool[nothing] = jnp.zeros(pool.shape[1:], pool.dtype)
    wanted = group * SLOTS
    for i in range(wanted):
        table[i] = nothing
    copy.wait()
    own_index = lax.axis_index("seq")
    for k in range(count):
        for b in range(blocks):
            member = label_ref[k, 2 * b] ^ own_index
            slot = label_ref[k, 2 * b + 1]
            table[jnp.where(member < group, member * SLOTS + slot, wanted)] = k * blocks + b
    for m in range(group):
        for s in range(SLOTS):
            outs[m][s] = pool[table[m * SLOTS + s]]


def route(parts, group, blocks):
    count = len(parts)
    chunk = BLOCK // group
    tiles = (parts[0].shape[0] - LABEL_ROWS) // (blocks * chunk)
    return pl.pallas_call(
        functools.partial(route_kernel, count, group, blocks),
        in_specs=[VMEM] * count,
        out_specs=[VMEM] * group,
        out_shape=[pltpu.VMEM((SLOTS, tiles, chunk, 128), jnp.bfloat16)] * group,
        scratch_shapes=[
            pltpu.VMEM((count * blocks + 1, tiles, chunk, 128), jnp.bfloat16),
            pltpu.VMEM((count, 128), jnp.int32),
            pltpu.SMEM((count, 128), jnp.int32),
            pltpu.SMEM((group * SLOTS + 1,), jnp.int32),
            pltpu.SemaphoreType.DMA,
        ],
        compiler_params=pltpu.CompilerParams(vmem_limit_bytes=VMEM_LIMIT),
        cost_estimate=pl.CostEstimate(
            flops=0,
            bytes_accessed=256 * (count * blocks + group * SLOTS) * tiles * chunk,
            transcendentals=0,
        ),
        name="route",
    )(*[near(part) for part in parts])


def join_kernel(members, *refs):
    out, sems = refs[-2:]
    parts = refs[: len(members)]
    _, tiles, chunk, _ = parts[0].shape
    own = lax.rem(lax.axis_index("seq"), BLOCK // chunk)
    copies = []
    for at, m in enumerate(members):
        start = pl.multiple_of((own ^ m) * chunk, chunk)
        for tile in range(tiles):
            there = out.at[:, pl.ds(start, chunk), tile * 128 : (tile + 1) * 128]
            copy = pltpu.make_async_copy(parts[at].at[:, tile], there, sems.at[at, tile])
            copy.start()
            copies.append(copy)
    for copy in copies:
        copy.wait()


def join(parts, members, before=None):
    slots, tiles, chunk, _ = parts[0].shape
    cols = tiles * 128
    operands = [near(part) for part in parts]
    in_specs = [VMEM] * len(parts)
    alias = {}
    if before is not None:
        operands.append(before)
        in_specs.append(ANY)
        alias = {len(parts): 0}
    return pl.pallas_call(
        functools.partial(join_kernel, members),
        in_specs=in_specs,
        out_specs=ANY,
        out_shape=jax.ShapeDtypeStruct((slots, BLOCK, cols), jnp.bfloat16),
        scratch_shapes=[pltpu.SemaphoreType.DMA((len(parts), tiles))],
        input_output_aliases=alias,
        compiler_params=pltpu.CompilerParams(vmem_limit_bytes=VMEM_LIMIT),
        cost_estimate=pl.CostEstimate(
            flops=0, bytes_accessed=4 * len(parts) * slots * chunk * cols, transcendentals=0
        ),
        name="join" if before is None else "join_last",
    )(*operands)


def per_device(seq_size, hidden, norm_gain, w_kv, lengths, page_table):
    seq_count, row_count, local_width = hidden.shape
    group = min(4, seq_size)
    flat = hidden.reshape(seq_count * row_count, local_width)
    other = lax.ppermute(flat, "tensor", [(0, 1), (1, 0)])

    def swap(array, k):
        return lax.ppermute(array, "seq", [(i, i ^ k) for i in range(seq_size)])

    gain = norm_gain.reshape(-1, 128)
    pages = page_table.reshape(-1)
    freq = frequencies()
    flat, freq = lax.optimization_barrier((flat, freq))
    acc, squares, far, gain, cosine, sine = first_half(flat, gain, w_kv, freq, row_count)
    outs = []

    def send(k):
        return swap(outs[k % group], k)

    shared = (lengths, pages, other, gain, far, acc, squares, cosine, sine, group)
    outs += second_half(*shared, (0,))
    parts = {k: send(k) for k in range(group, seq_size, group)}
    for members in (tuple(range(1, group)),):
        outs += second_half(*shared, members)
    parts[0] = outs[0]
    for k in range(1, seq_size):
        if k % group:
            parts[k] = send(k)
    sent = route([parts[k] for k in range(seq_size)], group, seq_count * row_count // BLOCK)
    placed = [sent[0]]
    for m in range(1, group):
        placed.append(swap(sent[m], m))
    members = tuple(range(group))
    kv_cache = join(placed[:-1], members[:-1])
    return join(placed[-1:], members[-1:], kv_cache)


def solution(mesh):
    placed = (P("group", "seq", "tensor"), P(), P(None, "tensor"), P("group"), P("group", "seq"))

    def body(*operands):
        return per_device(mesh.shape["seq"], *operands)

    return jax.shard_map(
        body,
        mesh=mesh,
        in_specs=placed,
        out_specs=P(("group", "seq"), None, "tensor"),
        check_vma=False,
    )
```

```python
import functools

import jax
import jax.numpy as jnp
from jax import lax
from jax.experimental import pallas as pl
from jax.experimental.pallas import tpu as pltpu
from jax.sharding import PartitionSpec as P


HD = 128
BLOCK = 128
SLOTS = 8
LABEL_ROWS = 8
DEPTH = 512
VMEM_LIMIT = 16 << 20


epsilon = 1e-05
rope_base = 500000.0


def frequencies():
    index = jnp.arange(HD, dtype=jnp.int32).reshape(1, HD) % (HD // 2)
    return rope_base ** (-2.0 * index.astype(jnp.float32) / HD)


VMEM = pl.BlockSpec(memory_space=pltpu.VMEM)
SMEM = pl.BlockSpec(memory_space=pltpu.SMEM)
ANY = pl.BlockSpec(memory_space=pl.ANY)
HBM = pl.BlockSpec(memory_space=pltpu.HBM)


def near(array):
    return pltpu.with_memory_space_constraint(array, pltpu.VMEM)


def far_away(array):
    return pltpu.with_memory_space_constraint(array, pltpu.HBM)


def lane_squares(x):
    wide = x.astype(jnp.float32)
    wide = wide * wide
    total = wide[:, :128]
    for c in range(1, x.shape[1] // 128):
        total += wide[:, c * 128 : (c + 1) * 128]
    return total


def scaled_by(x, gain_ref, row):
    parts = []
    for c in range(x.shape[1] // 128):
        gain = gain_ref[pl.ds(row + c, 1), :]
        wide = x[:, c * 128 : (c + 1) * 128].astype(jnp.float32) * gain
        parts.append(wide.astype(jnp.bfloat16))
    return jnp.concatenate(parts, axis=1)


def first_half_kernel(row_count, x_hbm, g_hbm, w_hbm, freq_ref, acc_ref, sq_ref, far_ref, gain, cos_ref, sin_ref, *scratch):
    g_buf, x_buf, w_buf, x_sem, w_sem, sems = scratch
    width = x_hbm.shape[1]
    steps = width // DEPTH
    side = lax.axis_index("tensor")
    near_row = pl.multiple_of(side * width, width)
    far_row = pl.multiple_of((1 - side) * width, width)
    copies = []
    for k in range(steps):
        span = slice(k * DEPTH, (k + 1) * DEPTH)
        copies.append(
            (
                pltpu.make_async_copy(x_hbm.at[:, span], x_buf.at[:, span], x_sem.at[k]),
                pltpu.make_async_copy(
                    w_hbm.at[pl.ds(near_row + k * DEPTH, DEPTH)], w_buf.at[span], w_sem.at[k]
                ),
            )
        )
    far = pltpu.make_async_copy(w_hbm.at[pl.ds(far_row, width)], far_ref, sems.at[0])
    gain_copy = pltpu.make_async_copy(g_hbm, g_buf, sems.at[1])
    gain_copy.start()
    for x_copy, w_copy in copies:
        x_copy.start()
        w_copy.start()
    far.start()
    first = lax.axis_index("seq") * row_count
    position = first + lax.broadcasted_iota(jnp.int32, cos_ref.shape, 0)
    angle = position.astype(jnp.float32) * freq_ref[...]
    cos_ref[...] = jnp.cos(angle)
    sine = jnp.sin(angle)
    lane = lax.broadcasted_iota(jnp.int32, sine.shape, 1)
    sin_ref[...] = jnp.where(lane < HD // 2, -sine, sine)
    gain_copy.wait()
    gain[...] = g_buf[...].astype(jnp.float32)
    for k in range(steps):
        for copy in copies[k]:
            copy.wait()
        span = slice(k * DEPTH, (k + 1) * DEPTH)
        x = x_buf[:, span]
        scaled = scaled_by(x, gain, side * (width // 128) + k * (DEPTH // 128))
        part = jnp.dot(scaled, w_buf[span], preferred_element_type=jnp.float32)
        squares = lane_squares(x)
        if k == 0:
            acc_ref[...] = part
            sq_ref[...] = squares
        else:
            acc_ref[...] += part
            sq_ref[...] += squares
    far.wait()


def first_half(x, gain, w, freq, row_count):
    rows, width = x.shape
    cols = w.shape[1]
    steps = width // DEPTH
    return pl.pallas_call(
        functools.partial(first_half_kernel, row_count),
        in_specs=[HBM, HBM, HBM, VMEM],
        out_specs=[VMEM] * 6,
        out_shape=[
            pltpu.VMEM((rows, cols), jnp.float32),
            pltpu.VMEM((rows, 128), jnp.float32),
            pltpu.VMEM((width, cols), jnp.bfloat16),
            pltpu.VMEM(gain.shape, jnp.float32),
            pltpu.VMEM((row_count, HD), jnp.float32),
            pltpu.VMEM((row_count, HD), jnp.float32),
        ],
        scratch_shapes=[
            pltpu.VMEM(gain.shape, jnp.bfloat16),
            pltpu.VMEM((rows, width), jnp.bfloat16),
            pltpu.VMEM((width, cols), jnp.bfloat16),
            pltpu.SemaphoreType.DMA((steps,)),
            pltpu.SemaphoreType.DMA((steps,)),
            pltpu.SemaphoreType.DMA((2,)),
        ],
        compiler_params=pltpu.CompilerParams(vmem_limit_bytes=VMEM_LIMIT),
        cost_estimate=pl.CostEstimate(
            flops=2 * rows * width * cols,
            bytes_accessed=2 * (rows * width + 2 * width * cols) + 4 * rows * cols,
            transcendentals=0,
        ),
        name="first_half",
    )(far_away(x), far_away(gain), far_away(w), freq)


def labels_of(page_ref):
    row = lax.broadcasted_iota(jnp.int32, (LABEL_ROWS, 128), 0)
    lane = lax.broadcasted_iota(jnp.int32, (LABEL_ROWS, 128), 1)
    tile = jnp.zeros((LABEL_ROWS, 128), jnp.int32)
    for b in range(page_ref.shape[0]):
        label = jnp.where(row == 0, page_ref[b] // SLOTS, page_ref[b] % SLOTS)
        tile = jnp.where(lane == b, label, tile)
    return tile.astype(jnp.float32).astype(jnp.bfloat16)


def second_half_kernel(group, members, len_ref, page_ref, x_ref, g_ref, w_ref, acc_in, sq_in, cos_ref, sin_ref, *outs):
    rows, width = x_ref.shape
    per_seq = cos_ref.shape[0]
    per = per_seq // BLOCK
    blocks = rows // BLOCK
    tiles = acc_in.shape[1] // 128
    chunk = BLOCK // group
    side = lax.axis_index("tensor")
    own_index = lax.axis_index("seq")
    own = lax.rem(own_index, group)

    def chunks(ref, columns):
        parts = []
        for m in members:
            for b in range(blocks):
                start = pl.multiple_of(b * BLOCK + (own ^ m) * chunk, chunk)
                parts.append(ref[pl.ds(start, chunk), columns])
        return jnp.concatenate(parts, axis=0)

    acc = chunks(acc_in, slice(None))
    squares = chunks(sq_in, slice(None))
    for k in range(width // DEPTH):
        span = slice(k * DEPTH, (k + 1) * DEPTH)
        x = chunks(x_ref, span)
        scaled = scaled_by(x, g_ref, (1 - side) * (width // 128) + k * (DEPTH // 128))
        acc += jnp.dot(scaled, w_ref[span, :], preferred_element_type=jnp.float32)
        squares += lane_squares(x)
    total = jnp.sum(squares, axis=-1, keepdims=True)
    inv = jnp.broadcast_to(lax.rsqrt(total / (2 * width) + epsilon), squares.shape)
    labels = labels_of(page_ref)
    for i, m in enumerate(members):
        for b in range(blocks):
            at = (i * blocks + b) * chunk
            band = slice(at, at + chunk)
            first = pl.multiple_of(b % per * BLOCK + (own ^ m) * chunk, chunk)
            row = own_index * per_seq + first + lax.broadcasted_iota(jnp.int32, (chunk, HD), 0)
            living = row < len_ref[b // per]
            cosine = cos_ref[pl.ds(first, chunk), :]
            sine = sin_ref[pl.ds(first, chunk), :]
            for tile in range(tiles):
                made = acc[band, tile * HD : (tile + 1) * HD] * inv[band]
                if tile % 2 == 0:
                    made = made * cosine + pltpu.roll(made, HD // 2, 1) * sine
                made = jnp.where(living, made, 0.0).astype(jnp.bfloat16)
                to = (b * tiles + tile) * chunk
                outs[i][to : to + chunk, :] = made
        outs[i][-LABEL_ROWS:, :] = labels


def second_half(lengths, pages, x, gain, w, acc, squares, cosine, sine, group, members):
    rows, width = x.shape
    cols = w.shape[1]
    height = rows // group * (cols // 128) + LABEL_ROWS
    count = rows // group * len(members)
    operands = [near(array) for array in (x, gain, w, acc, squares, cosine, sine)]
    return pl.pallas_call(
        functools.partial(second_half_kernel, group, members),
        in_specs=[SMEM] * 2 + [VMEM] * len(operands),
        out_specs=[VMEM] * len(members),
        out_shape=[pltpu.VMEM((height, 128), jnp.bfloat16)] * len(members),
        compiler_params=pltpu.CompilerParams(vmem_limit_bytes=VMEM_LIMIT),
        cost_estimate=pl.CostEstimate(
            flops=2 * count * width * cols,
            bytes_accessed=2 * width * (count + cols) + 4 * count * cols,
            transcendentals=0,
        ),
    )(lengths, pages, *operands)


def route_kernel(count, group, blocks, *refs):
    parts = refs[:count]
    outs = refs[count : count + group]
    pool, table = refs[count + group :]
    _, tiles, chunk, _ = pool.shape
    own_index = lax.axis_index("seq")
    wanted = group * SLOTS
    places = []
    for k in range(count):
        label = parts[k][-LABEL_ROWS:, :].astype(jnp.float32).astype(jnp.int32)
        member = label[0:1] ^ own_index
        places.append(jnp.where(member < group, member * SLOTS + label[1:2], wanted))
    for k in range(count):
        for b in range(blocks):
            for tile in range(tiles):
                row = (b * tiles + tile) * chunk
                pool[k * blocks + b, tile] = parts[k][row : row + chunk, :]
    nothing = count * blocks
    pool[nothing] = jnp.zeros(pool.shape[1:], pool.dtype)
    for i in range(wanted):
        table[i] = nothing
    for k in range(count):
        for b in range(blocks):
            table[places[k][0, b]] = k * blocks + b
    for m in range(group):
        for s in range(SLOTS):
            outs[m][s] = pool[table[m * SLOTS + s]]


def route(parts, group, blocks):
    count = len(parts)
    chunk = BLOCK // group
    tiles = (parts[0].shape[0] - LABEL_ROWS) // (blocks * chunk)
    return pl.pallas_call(
        functools.partial(route_kernel, count, group, blocks),
        in_specs=[VMEM] * count,
        out_specs=[VMEM] * group,
        out_shape=[pltpu.VMEM((SLOTS, tiles, chunk, 128), jnp.bfloat16)] * group,
        scratch_shapes=[
            pltpu.VMEM((count * blocks + 1, tiles, chunk, 128), jnp.bfloat16),
            pltpu.SMEM((group * SLOTS + 1,), jnp.int32),
        ],
        compiler_params=pltpu.CompilerParams(vmem_limit_bytes=VMEM_LIMIT),
        cost_estimate=pl.CostEstimate(
            flops=0,
            bytes_accessed=256 * (count * blocks + group * SLOTS) * tiles * chunk,
            transcendentals=0,
        ),
        name="route",
    )(*[near(part) for part in parts])


def join_kernel(members, *refs):
    out, sems = refs[-2:]
    parts = refs[: len(members)]
    _, tiles, chunk, _ = parts[0].shape
    own = lax.rem(lax.axis_index("seq"), BLOCK // chunk)
    copies = []
    for at, m in enumerate(members):
        start = pl.multiple_of((own ^ m) * chunk, chunk)
        for tile in range(tiles):
            there = out.at[:, pl.ds(start, chunk), tile * 128 : (tile + 1) * 128]
            copy = pltpu.make_async_copy(parts[at].at[:, tile], there, sems.at[at, tile])
            copy.start()
            copies.append(copy)
    for copy in copies:
        copy.wait()


def join(parts, members, before=None):
    slots, tiles, chunk, _ = parts[0].shape
    cols = tiles * 128
    operands = [near(part) for part in parts]
    in_specs = [VMEM] * len(parts)
    alias = {}
    if before is not None:
        operands.append(before)
        in_specs.append(ANY)
        alias = {len(parts): 0}
    return pl.pallas_call(
        functools.partial(join_kernel, members),
        in_specs=in_specs,
        out_specs=ANY,
        out_shape=jax.ShapeDtypeStruct((slots, BLOCK, cols), jnp.bfloat16),
        scratch_shapes=[pltpu.SemaphoreType.DMA((len(parts), tiles))],
        input_output_aliases=alias,
        compiler_params=pltpu.CompilerParams(vmem_limit_bytes=VMEM_LIMIT),
        cost_estimate=pl.CostEstimate(
            flops=0, bytes_accessed=4 * len(parts) * slots * chunk * cols, transcendentals=0
        ),
        name="join" if before is None else "join_last",
    )(*operands)


def per_device(seq_size, hidden, norm_gain, w_kv, lengths, page_table):
    seq_count, row_count, local_width = hidden.shape
    group = min(4, seq_size)
    flat = hidden.reshape(seq_count * row_count, local_width)
    other = lax.ppermute(flat, "tensor", [(0, 1), (1, 0)])

    def swap(array, k):
        return lax.ppermute(array, "seq", [(i, i ^ k) for i in range(seq_size)])

    gain = norm_gain.reshape(-1, 128)
    pages = page_table.reshape(-1)
    freq = frequencies()
    flat, freq = lax.optimization_barrier((flat, freq))
    acc, squares, far, gain, cosine, sine = first_half(flat, gain, w_kv, freq, row_count)
    outs = []

    def send(k):
        return swap(outs[k % group], k)

    shared = (lengths, pages, other, gain, far, acc, squares, cosine, sine, group)
    outs += second_half(*shared, (0,))
    parts = {k: send(k) for k in range(group, seq_size, group)}
    for members in (tuple(range(1, group)),):
        outs += second_half(*shared, members)
    parts[0] = outs[0]
    for k in range(1, seq_size):
        if k % group:
            parts[k] = send(k)
    sent = route([parts[k] for k in range(seq_size)], group, seq_count * row_count // BLOCK)
    placed = [sent[0]]
    for m in range(1, group):
        placed.append(swap(sent[m], m))
    members = tuple(range(group))
    kv_cache = join(placed[:-1], members[:-1])
    return join(placed[-1:], members[-1:], kv_cache)


def solution(mesh):
    placed = (P("group", "seq", "tensor"), P(), P(None, "tensor"), P("group"), P("group", "seq"))

    def body(*operands):
        return per_device(mesh.shape["seq"], *operands)

    return jax.shard_map(
        body,
        mesh=mesh,
        in_specs=placed,
        out_specs=P(("group", "seq"), None, "tensor"),
        check_vma=False,
    )
```

```python
import functools

import jax
import jax.numpy as jnp
from jax import lax
from jax.experimental import pallas as pl
from jax.experimental.pallas import tpu as pltpu
from jax.sharding import PartitionSpec as P


HD = 128
BLOCK = 128
SLOTS = 8
LABEL_ROWS = 8
DEPTH = 512
VMEM_LIMIT = 16 << 20


epsilon = 1e-05
rope_base = 500000.0


def frequencies():
    index = jnp.arange(HD, dtype=jnp.int32).reshape(1, HD) % (HD // 2)
    return rope_base ** (-2.0 * index.astype(jnp.float32) / HD)


VMEM = pl.BlockSpec(memory_space=pltpu.VMEM)
SMEM = pl.BlockSpec(memory_space=pltpu.SMEM)
ANY = pl.BlockSpec(memory_space=pl.ANY)
HBM = pl.BlockSpec(memory_space=pltpu.HBM)


def near(array):
    return pltpu.with_memory_space_constraint(array, pltpu.VMEM)


def far_away(array):
    return pltpu.with_memory_space_constraint(array, pltpu.HBM)


def lane_squares(x):
    wide = x.astype(jnp.float32)
    wide = wide * wide
    total = wide[:, :128]
    for c in range(1, x.shape[1] // 128):
        total += wide[:, c * 128 : (c + 1) * 128]
    return total


def scaled_by(x, gain_ref, row):
    parts = []
    for c in range(x.shape[1] // 128):
        gain = gain_ref[pl.ds(row + c, 1), :]
        wide = x[:, c * 128 : (c + 1) * 128].astype(jnp.float32) * gain
        parts.append(wide.astype(jnp.bfloat16))
    return jnp.concatenate(parts, axis=1)


def first_half_kernel(row_count, x_hbm, g_hbm, w_hbm, freq_ref, acc_ref, sq_ref, far_ref, gain, cos_ref, sin_ref, *scratch):
    g_buf, x_buf, w_buf, x_sem, w_sem, sems = scratch
    width = x_hbm.shape[1]
    steps = width // DEPTH
    side = lax.axis_index("tensor")
    near_row = pl.multiple_of(side * width, width)
    far_row = pl.multiple_of((1 - side) * width, width)
    copies = []
    for k in range(steps):
        span = slice(k * DEPTH, (k + 1) * DEPTH)
        copies.append(
            (
                pltpu.make_async_copy(x_hbm.at[:, span], x_buf.at[:, span], x_sem.at[k]),
                pltpu.make_async_copy(
                    w_hbm.at[pl.ds(near_row + k * DEPTH, DEPTH)], w_buf.at[span], w_sem.at[k]
                ),
            )
        )
    far = pltpu.make_async_copy(w_hbm.at[pl.ds(far_row, width)], far_ref, sems.at[0])
    gain_copy = pltpu.make_async_copy(g_hbm, g_buf, sems.at[1])
    gain_copy.start()
    for x_copy, w_copy in copies:
        x_copy.start()
        w_copy.start()
    far.start()
    first = lax.axis_index("seq") * row_count
    position = first + lax.broadcasted_iota(jnp.int32, cos_ref.shape, 0)
    angle = position.astype(jnp.float32) * freq_ref[...]
    cos_ref[...] = jnp.cos(angle)
    sine = jnp.sin(angle)
    lane = lax.broadcasted_iota(jnp.int32, sine.shape, 1)
    sin_ref[...] = jnp.where(lane < HD // 2, -sine, sine)
    gain_copy.wait()
    gain[...] = g_buf[...].astype(jnp.float32)
    for k in range(steps):
        for copy in copies[k]:
            copy.wait()
        span = slice(k * DEPTH, (k + 1) * DEPTH)
        x = x_buf[:, span]
        scaled = scaled_by(x, gain, side * (width // 128) + k * (DEPTH // 128))
        part = jnp.dot(scaled, w_buf[span], preferred_element_type=jnp.float32)
        squares = lane_squares(x)
        if k == 0:
            acc_ref[...] = part
            sq_ref[...] = squares
        else:
            acc_ref[...] += part
            sq_ref[...] += squares
    far.wait()


def first_half(x, gain, w, freq, row_count):
    rows, width = x.shape
    cols = w.shape[1]
    steps = width // DEPTH
    return pl.pallas_call(
        functools.partial(first_half_kernel, row_count),
        in_specs=[HBM, HBM, HBM, VMEM],
        out_specs=[VMEM] * 6,
        out_shape=[
            pltpu.VMEM((rows, cols), jnp.float32),
            pltpu.VMEM((rows, 128), jnp.float32),
            pltpu.VMEM((width, cols), jnp.bfloat16),
            pltpu.VMEM(gain.shape, jnp.float32),
            pltpu.VMEM((row_count, HD), jnp.float32),
            pltpu.VMEM((row_count, HD), jnp.float32),
        ],
        scratch_shapes=[
            pltpu.VMEM(gain.shape, jnp.bfloat16),
            pltpu.VMEM((rows, width), jnp.bfloat16),
            pltpu.VMEM((width, cols), jnp.bfloat16),
            pltpu.SemaphoreType.DMA((steps,)),
            pltpu.SemaphoreType.DMA((steps,)),
            pltpu.SemaphoreType.DMA((2,)),
        ],
        compiler_params=pltpu.CompilerParams(vmem_limit_bytes=VMEM_LIMIT),
        cost_estimate=pl.CostEstimate(
            flops=2 * rows * width * cols,
            bytes_accessed=2 * (rows * width + 2 * width * cols) + 4 * rows * cols,
            transcendentals=0,
        ),
        name="first_half",
    )(far_away(x), far_away(gain), far_away(w), freq)


def labels_of(page_ref):
    row = lax.broadcasted_iota(jnp.int32, (LABEL_ROWS, 128), 0)
    lane = lax.broadcasted_iota(jnp.int32, (LABEL_ROWS, 128), 1)
    tile = jnp.zeros((LABEL_ROWS, 128), jnp.int32)
    for b in range(page_ref.shape[0]):
        label = jnp.where(row == 0, page_ref[b] // SLOTS, page_ref[b] % SLOTS)
        tile = jnp.where(lane == b, label, tile)
    return tile.astype(jnp.float32).astype(jnp.bfloat16)


def second_half_kernel(group, members, len_ref, page_ref, x_ref, g_ref, w_ref, acc_in, sq_in, cos_ref, sin_ref, *outs):
    rows, width = x_ref.shape
    per_seq = cos_ref.shape[0]
    per = per_seq // BLOCK
    blocks = rows // BLOCK
    tiles = acc_in.shape[1] // 128
    chunk = BLOCK // group
    side = lax.axis_index("tensor")
    own_index = lax.axis_index("seq")
    own = lax.rem(own_index, group)

    def chunks(ref, columns):
        parts = []
        for m in members:
            for b in range(blocks):
                start = pl.multiple_of(b * BLOCK + (own ^ m) * chunk, chunk)
                parts.append(ref[pl.ds(start, chunk), columns])
        return jnp.concatenate(parts, axis=0)

    acc = chunks(acc_in, slice(None))
    squares = chunks(sq_in, slice(None))
    for k in range(width // DEPTH):
        span = slice(k * DEPTH, (k + 1) * DEPTH)
        x = chunks(x_ref, span)
        scaled = scaled_by(x, g_ref, (1 - side) * (width // 128) + k * (DEPTH // 128))
        acc += jnp.dot(scaled, w_ref[span, :], preferred_element_type=jnp.float32)
        squares += lane_squares(x)
    total = jnp.sum(squares, axis=-1, keepdims=True)
    inv = jnp.broadcast_to(lax.rsqrt(total / (2 * width) + epsilon), squares.shape)
    labels = labels_of(page_ref)
    for i, m in enumerate(members):
        for b in range(blocks):
            at = (i * blocks + b) * chunk
            band = slice(at, at + chunk)
            first = pl.multiple_of(b % per * BLOCK + (own ^ m) * chunk, chunk)
            row = own_index * per_seq + first + lax.broadcasted_iota(jnp.int32, (chunk, HD), 0)
            living = row < len_ref[b // per]
            cosine = cos_ref[pl.ds(first, chunk), :]
            sine = sin_ref[pl.ds(first, chunk), :]
            for tile in range(tiles):
                made = acc[band, tile * HD : (tile + 1) * HD] * inv[band]
                if tile % 2 == 0:
                    made = made * cosine + pltpu.roll(made, HD // 2, 1) * sine
                made = jnp.where(living, made, 0.0).astype(jnp.bfloat16)
                to = (b * tiles + tile) * chunk
                outs[i][to : to + chunk, :] = made
        outs[i][-LABEL_ROWS:, :] = labels


def second_half(lengths, pages, x, gain, w, acc, squares, cosine, sine, group, members):
    rows, width = x.shape
    cols = w.shape[1]
    height = rows // group * (cols // 128) + LABEL_ROWS
    count = rows // group * len(members)
    operands = [near(array) for array in (x, gain, w, acc, squares, cosine, sine)]
    return pl.pallas_call(
        functools.partial(second_half_kernel, group, members),
        in_specs=[SMEM] * 2 + [VMEM] * len(operands),
        out_specs=[VMEM] * len(members),
        out_shape=[pltpu.VMEM((height, 128), jnp.bfloat16)] * len(members),
        compiler_params=pltpu.CompilerParams(vmem_limit_bytes=VMEM_LIMIT),
        cost_estimate=pl.CostEstimate(
            flops=2 * count * width * cols,
            bytes_accessed=2 * width * (count + cols) + 4 * count * cols,
            transcendentals=0,
        ),
    )(lengths, pages, *operands)


def route_kernel(count, group, blocks, *refs):
    parts = refs[:count]
    outs = refs[count : count + group + 1]
    pool, table = refs[count + group + 1 :]
    _, tiles, chunk, _ = pool.shape
    own_index = lax.axis_index("seq")
    wanted = group * SLOTS
    places = []
    for k in range(count):
        label = parts[k][-LABEL_ROWS:, :].astype(jnp.float32).astype(jnp.int32)
        member = label[0:1] ^ own_index
        places.append(jnp.where(member < group, member * SLOTS + label[1:2], wanted))
    for k in range(count):
        for b in range(blocks):
            for tile in range(tiles):
                row = (b * tiles + tile) * chunk
                pool[k * blocks + b, tile] = parts[k][row : row + chunk, :]
    nothing = count * blocks
    pool[nothing] = jnp.zeros(pool.shape[1:], pool.dtype)
    for i in range(wanted):
        table[i] = nothing
    for k in range(count):
        for b in range(blocks):
            table[places[k][0, b]] = k * blocks + b
    for m in range(group):
        for s in range(SLOTS):
            if m == group - 1 and s >= SLOTS // 2:
                outs[group][s - SLOTS // 2] = pool[table[m * SLOTS + s]]
            else:
                outs[m][s] = pool[table[m * SLOTS + s]]


def route(parts, group, blocks):
    count = len(parts)
    chunk = BLOCK // group
    tiles = (parts[0].shape[0] - LABEL_ROWS) // (blocks * chunk)
    return pl.pallas_call(
        functools.partial(route_kernel, count, group, blocks),
        in_specs=[VMEM] * count,
        out_specs=[VMEM] * (group + 1),
        out_shape=[
            pltpu.VMEM((slots, tiles, chunk, 128), jnp.bfloat16)
            for slots in [SLOTS] * (group - 1) + [SLOTS // 2, SLOTS - SLOTS // 2]
        ],
        scratch_shapes=[
            pltpu.VMEM((count * blocks + 1, tiles, chunk, 128), jnp.bfloat16),
            pltpu.SMEM((group * SLOTS + 1,), jnp.int32),
        ],
        compiler_params=pltpu.CompilerParams(vmem_limit_bytes=VMEM_LIMIT),
        cost_estimate=pl.CostEstimate(
            flops=0,
            bytes_accessed=256 * (count * blocks + group * SLOTS) * tiles * chunk,
            transcendentals=0,
        ),
        name="route",
    )(*[near(part) for part in parts])


def join_kernel(members, *refs):
    out, sems = refs[-2:]
    parts = refs[: len(members)]
    _, tiles, chunk, _ = parts[0].shape
    own = lax.rem(lax.axis_index("seq"), BLOCK // chunk)
    copies = []
    for at, (m, slot) in enumerate(members):
        start = pl.multiple_of((own ^ m) * chunk, chunk)
        for tile in range(tiles):
            slots = pl.ds(slot, parts[at].shape[0])
            there = out.at[slots, pl.ds(start, chunk), tile * 128 : (tile + 1) * 128]
            copy = pltpu.make_async_copy(parts[at].at[:, tile], there, sems.at[at, tile])
            copy.start()
            copies.append(copy)
    for copy in copies:
        copy.wait()


def join(parts, members, before=None):
    _, tiles, chunk, _ = parts[0].shape
    slots = SLOTS
    cols = tiles * 128
    operands = [near(part) for part in parts]
    in_specs = [VMEM] * len(parts)
    alias = {}
    if before is not None:
        operands.append(before)
        in_specs.append(ANY)
        alias = {len(parts): 0}
    return pl.pallas_call(
        functools.partial(join_kernel, members),
        in_specs=in_specs,
        out_specs=ANY,
        out_shape=jax.ShapeDtypeStruct((slots, BLOCK, cols), jnp.bfloat16),
        scratch_shapes=[pltpu.SemaphoreType.DMA((len(parts), tiles))],
        input_output_aliases=alias,
        compiler_params=pltpu.CompilerParams(vmem_limit_bytes=VMEM_LIMIT),
        cost_estimate=pl.CostEstimate(
            flops=0, bytes_accessed=4 * len(parts) * slots * chunk * cols, transcendentals=0
        ),
        name="join" if before is None else "join_last",
    )(*operands)


def per_device(seq_size, hidden, norm_gain, w_kv, lengths, page_table):
    seq_count, row_count, local_width = hidden.shape
    group = min(4, seq_size)
    flat = hidden.reshape(seq_count * row_count, local_width)
    other = lax.ppermute(flat, "tensor", [(0, 1), (1, 0)])

    def swap(array, k):
        return lax.ppermute(array, "seq", [(i, i ^ k) for i in range(seq_size)])

    gain = norm_gain.reshape(-1, 128)
    pages = page_table.reshape(-1)
    freq = frequencies()
    flat, freq = lax.optimization_barrier((flat, freq))
    acc, squares, far, gain, cosine, sine = first_half(flat, gain, w_kv, freq, row_count)
    outs = []

    def send(k):
        return swap(outs[k % group], k)

    shared = (lengths, pages, other, gain, far, acc, squares, cosine, sine, group)
    outs += second_half(*shared, (0,))
    parts = {k: send(k) for k in range(group, seq_size, group)}
    for members in (tuple(range(1, group)),):
        outs += second_half(*shared, members)
    parts[0] = outs[0]
    for k in range(1, seq_size):
        if k % group:
            parts[k] = send(k)
    sent = route([parts[k] for k in range(seq_size)], group, seq_count * row_count // BLOCK)
    placed = [sent[0]]
    for m in range(1, group):
        placed.append(swap(sent[m], m))
    placed.append(swap(sent[group], group - 1))
    members = [(m, 0) for m in range(group)] + [(group - 1, SLOTS // 2)]
    kv_cache = join(placed[:4], members[:4])
    return join(placed[4:], members[4:], kv_cache)


def solution(mesh):
    placed = (P("group", "seq", "tensor"), P(), P(None, "tensor"), P("group"), P("group", "seq"))

    def body(*operands):
        return per_device(mesh.shape["seq"], *operands)

    return jax.shard_map(
        body,
        mesh=mesh,
        in_specs=placed,
        out_specs=P(("group", "seq"), None, "tensor"),
        check_vma=False,
    )
```
